256 devices in a mesh: seq: 32 (over y, z), grp: 8 (over x, core).
Axes of the slice: x: 4, y: 4, z: 8, core: 2. Of those that a mesh axis runs over, the one named last changes fastest.
Arguments:
- hidden: bfloat16 [16384, 2048], P('seq', 'grp'), may hold values from -8 to 8
- qkv_weight: bfloat16 [3, 2048, 6144], P(None, 'seq', 'grp'), may hold values from -0.125 to 0.125
- out_weight: bfloat16 [3, 2048, 2048], P(None, 'grp', 'seq'), may hold values from -0.125 to 0.125
- projection: float32 [3, 16, 128, 128], P(None, 'grp'), may hold values from -6 to 6
- norm_gain: float32 [3, 2048], replicated, may hold values from 0.1 to 1.9
- out_gain: float32 [3, 2048], P(None, 'grp'), may hold values from 0.1 to 1.9
Outputs:
- layer_out: bfloat16 [16384, 2048], P('seq', 'grp')
The draws below stay inside these ranges and needn't reach their ends.
All inputs are finite; a program needn't handle non-finite values.
Results may differ from the reference program's by a relative error of at most 0.034.
Values may be sent and summed in bfloat16 or wider, within the bound.
No kernel may reach another device: no remote copies, remote signals or barrier semaphores. Data moves between devices by JAX's collectives and lax.ppermute only.
A program may use at most 64 MiB of HBM per device.

```python
import math
import jax
import jax.numpy as jnp
from jax import lax

D = 2048
H = 16
E = 128
M = 128
LAYERS = 3
TOK_DEV = 512
TOKENS = 16384
N_GRP = 8


def draw_hidden(key, part):
    base = jax.random.normal(jax.random.fold_in(key, 11), (TOKENS, D), jnp.float32)
    return jnp.clip(base, -8.0, 8.0).astype(jnp.bfloat16)


def block_scale(key, extent, shards, least, high):
    gain = 1.0
    for position, blocks in shards:
        heights = jax.random.uniform(jax.random.fold_in(jax.random.fold_in(key, 6), position), (blocks,), jnp.float32, least / len(shards), high / len(shards))
        gain = gain * jnp.repeat(jnp.exp(heights), extent[position] // blocks).reshape((-1,) + (1,) * (len(extent) - 1 - position))
    return gain


def normal_values(key, shape, scale, limit, pieces=(), held_as=jnp.bfloat16):
    gain = block_scale(key, shape, pieces, -0.22, 0.18) if pieces else 1.0
    drawn = jax.random.normal(key, shape, jnp.float32) * scale * gain
    return jnp.minimum(jnp.maximum(drawn, -limit), limit).astype(held_as)


def setup_inputs(seed: int = 0) -> dict:
    splits = jax.random.split(jax.random.key(seed), 7)
    hidden = draw_hidden(jax.random.fold_in(splits[6], 71), 0)
    qkv_weight = normal_values(splits[1], (LAYERS, D, 3 * H * E), D ** -0.5, 0.125, ((1, 32), (2, 8)))
    out_weight = normal_values(splits[2], (LAYERS, H * E, D), (H * E) ** -0.5, 0.125, ((1, 8), (2, 32)))
    projection = normal_values(splits[3], (LAYERS, H, E, M), 1.0, 6.0, ((1, 8),), jnp.float32)
    norm_gain = jnp.clip(1.0 + 0.18 * jax.random.normal(splits[4], (LAYERS, D), jnp.float32), 0.1, 1.9)
    out_gain = jnp.clip(1.0 + 0.18 * jax.random.normal(splits[5], (LAYERS, H * E), jnp.float32), 0.1, 1.9)
    return {"hidden": hidden, "qkv_weight": qkv_weight, "out_weight": out_weight, "projection": projection, "norm_gain": norm_gain, "out_gain": out_gain}


stabilizer = 2.0
highest = lax.Precision.HIGHEST

def features(rows, projection_layer):
    scaled = rows.astype(jnp.float32) * E ** (-0.25)
    mixed = jnp.einsum('thd,hdm->thm', scaled, projection_layer, precision=highest)
    energy = 0.5 * lax.optimization_barrier(jnp.sum(scaled * scaled, axis=-1, keepdims=True))
    return (jnp.exp(mixed - energy - stabilizer) / math.sqrt(M)).astype(jnp.bfloat16)

def block_step(carried, block):
    prefix_kv, prefix_z = carried
    query_feat, key_feat, value_rows = block
    query_wide = query_feat.astype(jnp.float32)
    key_wide = key_feat.astype(jnp.float32)
    value_wide = value_rows.astype(jnp.float32)
    scores = jnp.einsum('ihm,jhm->hij', query_wide, key_wide, precision=highest)
    count = scores.shape[-1]
    causal_mask = jnp.arange(count)[:, None] >= jnp.arange(count)[None, :]
    masked = jnp.where(causal_mask[None], scores, jnp.zeros_like(scores))
    score_weights = lax.optimization_barrier(masked.astype(jnp.bfloat16)).astype(jnp.float32)
    rounded_kv = lax.optimization_barrier(prefix_kv.astype(jnp.bfloat16)).astype(jnp.float32)
    denominator = lax.optimization_barrier(jnp.sum(masked, axis=-1)) + jnp.einsum('ihm,hm->hi', query_wide, prefix_z, precision=highest)
    numerator = jnp.einsum('hij,jhe->hie', score_weights, value_wide, precision=highest)
    numerator = numerator + jnp.einsum('ihm,hme->hie', query_wide, rounded_kv, precision=highest)
    attention = numerator / denominator[..., None]
    block_kv = jnp.einsum('jhm,jhe->hme', key_wide, value_wide, precision=highest)
    block_z = lax.optimization_barrier(jnp.sum(key_wide, axis=0))
    return ((prefix_kv + block_kv, prefix_z + block_z), jnp.transpose(attention, (1, 0, 2)))

def reference(hidden, qkv_weight, out_weight, projection, norm_gain, out_gain):
    stream = hidden
    blocks = TOKENS // TOK_DEV
    group_cols = H // N_GRP * E
    for layer_index in range(LAYERS):
        wide = stream.astype(jnp.float32)
        inverse_rms = lax.rsqrt(lax.optimization_barrier(jnp.mean(wide * wide, axis=-1, keepdims=True)) + 1e-05)
        normed = (wide * inverse_rms * norm_gain[layer_index][None, :]).astype(jnp.bfloat16)
        qkv = jnp.dot(normed, qkv_weight[layer_index], preferred_element_type=jnp.float32).astype(jnp.bfloat16)
        qkv = qkv.reshape(TOKENS, H, 3, E)
        query_feat = features(qkv[:, :, 0], projection[layer_index])
        key_feat = features(qkv[:, :, 1], projection[layer_index])
        value_rows = qkv[:, :, 2]
        start_state = (jnp.zeros((H, M, E), jnp.float32), jnp.zeros((H, M), jnp.float32))
        packed = (query_feat.reshape(blocks, TOK_DEV, H, M), key_feat.reshape(blocks, TOK_DEV, H, M), value_rows.reshape(blocks, TOK_DEV, H, E))
        final_state, attention = lax.scan(block_step, start_state, packed)
        attention = attention.reshape(TOKENS, H, E)
        inverse_norm = lax.rsqrt(lax.optimization_barrier(jnp.mean(attention * attention, axis=-1, keepdims=True)) + 1e-06)
        attended = (attention * inverse_norm * out_gain[layer_index].reshape(H, E)[None]).astype(jnp.bfloat16)
        attended = attended.reshape(TOKENS, H * E)
        summed = jnp.zeros((TOKENS, D), jnp.float32)
        for group_index in range(N_GRP):
            lower = group_index * group_cols
            partial_value = jnp.dot(attended[:, lower:lower + group_cols], out_weight[layer_index][lower:lower + group_cols], preferred_element_type=jnp.float32)
            summed = summed + lax.optimization_barrier(partial_value.astype(jnp.bfloat16)).astype(jnp.float32)
        stream = (stream.astype(jnp.float32) + summed).astype(jnp.bfloat16)
    return stream
```

```python
import jax
import jax.numpy as jnp
from jax import lax
from jax.experimental import pallas as pl
from jax.experimental.pallas import tpu as pltpu
from jax.sharding import Mesh
from jax.sharding import PartitionSpec as P

SEQ = ("y", "z")
GRP = ("x", "c")
X = 4
STABILIZER = 2.0
bf16, f32 = jnp.bfloat16, jnp.float32
VMEM = pl.BlockSpec(memory_space=pltpu.VMEM)
SMEM = pl.BlockSpec(memory_space=pltpu.SMEM)
ANY = pl.BlockSpec(memory_space=pl.ANY)

FORWARD = [(2 * x + c, 2 * ((x + (1 - 2 * c)) % X) + c) for x in range(X) for c in range(2)]
BACKWARD = [(b, a) for a, b in FORWARD]
SWAP = [(0, 1), (1, 0)]


def swap(a):
    return lax.ppermute(a, "c", SWAP)


def group_ids():
    x, c = lax.axis_index("x"), lax.axis_index("c")
    s, d = 1 - 2 * c, 1 - c
    at = lambda i, core: (i + X) % X * 2 + core
    came = [at(x, c), at(x - s, c), at(x + s, c), at(x + 2, c), at(x, d), at(x + s, d), at(x - s, d), at(x + 2, d)]
    goes = [at(x + 2, c), at(x + s, c), at(x - s, c), at(x, c), at(x + 2, d), at(x - s, d), at(x + s, d), at(x, d)]
    return jnp.stack(came + goes).astype(jnp.int32)


def dot(a, b, dims=((1,), (0,))):
    return lax.dot_general(a, b, (dims, ((), ())), preferred_element_type=f32)


def project_kernel(layer, ids, *refs):
    parts = refs[:8]
    gain, w_hbm, proj, qf_ref, kf_ref, v_ref, state_ref, w, sem = refs[8:]
    copies = []
    for k in range(8):
        rows = pl.ds(pl.multiple_of(ids[k] * 256, 256), 256)
        copies.append(
            pltpu.make_async_copy(w_hbm.at[rows, pl.ds(0, 768)], w.at[pl.ds(k * 256, 256)], sem.at[k])
        )
        copies[-1].start()
    tokens = parts[0].shape[0]
    squares = jnp.zeros((tokens, 256), f32)
    acc = jnp.zeros((tokens, 768), f32)
    for k in range(8):
        wide = parts[k][...].astype(f32)
        squares += wide * wide
        scaled = (wide * gain[pl.ds(layer * 8 + ids[k], 1), :]).astype(bf16)
        copies[k].wait()
        acc += dot(scaled, w[pl.ds(k * 256, 256), :])
    inverse_rms = lax.rsqrt(jnp.sum(squares, axis=-1, keepdims=True) * (1.0 / 2048) + 1e-05)
    qkv = (acc * inverse_rms).astype(bf16)
    ones = jnp.ones((tokens, 128), bf16)
    for n in range(2):
        scaled = proj[layer, n] * 128 ** (-0.25)
        high = scaled.astype(bf16)
        rest = scaled - high.astype(f32)
        mid = rest.astype(bf16)
        low = (rest - mid.astype(f32)).astype(bf16)
        pair = jnp.concatenate([high, mid], axis=1)
        feats = []
        for j in range(2):
            u = qkv[:, n * 384 + j * 128 : n * 384 + (j + 1) * 128]
            both = dot(u, pair)
            mixed = both[:, :128] + (both[:, 128:] + dot(u, low))
            uw = u.astype(f32)
            energy = jnp.sum(uw * uw, axis=-1, keepdims=True) * (0.5 * 128 ** (-0.5))
            feats.append((jnp.exp(mixed - energy - STABILIZER) * 128 ** (-0.5)).astype(bf16))
        value = qkv[:, n * 384 + 256 : n * 384 + 384]
        cols = pl.ds(n * 128, 128)
        qf_ref[:, cols] = feats[0]
        kf_ref[:, cols] = feats[1]
        v_ref[:, cols] = value
        with_ones = jnp.concatenate([value, ones], axis=1)
        state_ref[cols, :] = dot(feats[1], with_ones, ((0,), (0,))).astype(bf16)


def project(layer, ids, parts, gain, w, proj):
    tokens = parts[0].shape[0]
    half = jax.ShapeDtypeStruct((tokens, 256), bf16)
    return pl.pallas_call(
        lambda *refs: project_kernel(layer, *refs),
        name="project",
        out_shape=(half, half, half, jax.ShapeDtypeStruct((256, 256), bf16)),
        in_specs=[SMEM] + [VMEM] * 9 + [ANY, VMEM],
        out_specs=(VMEM,) * 4,
        scratch_shapes=[pltpu.VMEM((2048, 768), bf16), pltpu.SemaphoreType.DMA((8,))],
        cost_estimate=pl.CostEstimate(flops=2 * 512 * 2048 * 768, bytes_accessed=6 * 2**20, transcendentals=0),
        compiler_params=pltpu.CompilerParams(vmem_limit_bytes=40 * 2**20),
    )(ids, *parts, gain, w, proj)


def local_kernel(qf, kf, v, num_ref, den_ref):
    tile = 256
    keep = lax.broadcasted_iota(jnp.int32, (tile, tile), 0) >= lax.broadcasted_iota(jnp.int32, (tile, tile), 1)
    for n in range(2):
        cols = pl.ds(n * 128, 128)
        for i in range(qf.shape[0] // tile):
            rows = pl.ds(i * tile, tile)
            num = jnp.zeros((tile, 128), f32)
            den = jnp.zeros((tile, 1), f32)
            for j in range(i + 1):
                keys = pl.ds(j * tile, tile)
                scores = dot(qf[rows, cols], kf[keys, cols], ((1,), (1,)))
                if j == i:
                    scores = jnp.where(keep, scores, 0.0)
                den += jnp.sum(scores, axis=-1, keepdims=True)
                num += dot(scores.astype(bf16), v[keys, cols])
            num_ref[rows, cols] = num
            den_ref[rows, cols] = jnp.broadcast_to(den, (tile, 128))


def local_attention(qf, kf, v):
    whole = jax.ShapeDtypeStruct(qf.shape, f32)
    return pl.pallas_call(
        local_kernel,
        name="local_attention",
        out_shape=(whole, whole),
        in_specs=[VMEM] * 3,
        out_specs=(VMEM,) * 2,
        cost_estimate=pl.CostEstimate(flops=2 * 4 * 512 * 512 * 128, bytes_accessed=2 * 2**20, transcendentals=0),
        compiler_params=pltpu.CompilerParams(vmem_limit_bytes=32 * 2**20),
    )(qf, kf, v)


def prefix_kernel(in_ref, out_ref):
    total = jnp.zeros(in_ref.shape[1:], f32)
    for s in range(in_ref.shape[0]):
        out_ref[s] = total.astype(bf16)
        total += in_ref[s].astype(f32)


def prefix(slices):
    return pl.pallas_call(
        prefix_kernel,
        name="prefix",
        out_shape=jax.ShapeDtypeStruct(slices.shape, bf16),
        in_specs=[VMEM],
        out_specs=VMEM,
    )(slices)


def finish_kernel(layer, ids, qf, num, den, before, gain, w_hbm, *refs):
    outs = refs[:8]
    w, sem = refs[8:]
    copies = []
    for k in range(8):
        rows = pl.ds(pl.multiple_of(ids[8 + k] * 256, 256), 256)
        copies.append(
            pltpu.make_async_copy(w_hbm.at[rows, pl.ds(768, 256)], w.at[pl.ds(k * 256, 256)], sem.at[k])
        )
        copies[-1].start()
    heads = []
    for n in range(2):
        cols = pl.ds(n * 128, 128)
        both = dot(qf[:, cols], before[cols, :])
        attention = (num[:, cols] + both[:, :128]) / (den[:, cols] + both[:, 128:])
        inverse = lax.rsqrt(jnp.sum(attention * attention, axis=-1, keepdims=True) * (1.0 / 128) + 1e-06)
        heads.append((attention * inverse * gain[pl.ds(layer, 1), cols]).astype(bf16))
    attended = jnp.concatenate(heads, axis=1)
    for k in range(8):
        copies[k].wait()
        outs[k][...] = dot(attended, w[pl.ds(k * 256, 256), :], ((1,), (1,))).astype(bf16)


def finish(layer, ids, qf, num, den, before, gain, w):
    part = jax.ShapeDtypeStruct(qf.shape, bf16)
    return pl.pallas_call(
        lambda *refs: finish_kernel(layer, *refs),
        name="finish",
        out_shape=(part,) * 8,
        in_specs=[SMEM] + [VMEM] * 5 + [ANY],
        out_specs=(VMEM,) * 8,
        scratch_shapes=[pltpu.VMEM((2048, 256), bf16), pltpu.SemaphoreType.DMA((8,))],
        cost_estimate=pl.CostEstimate(flops=2 * 512 * 256 * 2304, bytes_accessed=5 * 2**20, transcendentals=0),
        compiler_params=pltpu.CompilerParams(vmem_limit_bytes=32 * 2**20),
    )(ids, qf, num, den, before, gain, w)


def gathered(own):
    a = lax.ppermute(own, GRP, FORWARD)
    b = lax.ppermute(own, GRP, BACKWARD)
    o = lax.ppermute(a, GRP, FORWARD)
    mine = [own, a, b, o]
    return mine + [swap(p) for p in mine]


def scattered(outs):
    mine, other = outs[:4], outs[4:]
    far, near, back, own = [
        (m.astype(f32) + swap(o).astype(f32)) for m, o in zip(mine, other)
    ]
    relayed = lax.ppermute(far.astype(bf16), GRP, FORWARD)
    b = lax.ppermute(back.astype(bf16), GRP, BACKWARD)
    a = lax.ppermute((near + relayed.astype(f32)).astype(bf16), GRP, FORWARD)
    return own + b.astype(f32) + a.astype(f32)


def local(hidden, qkv_weight, out_weight, projection, norm_gain, out_gain):
    layers = qkv_weight.shape[0]
    out_t = jnp.swapaxes(out_weight, 1, 2)
    shards = [jnp.concatenate([qkv_weight[l], out_t[l]], axis=1) for l in range(layers)]
    first = lax.all_gather(shards[0], SEQ, axis=0, tiled=True)
    later = [lax.all_gather(s, SEQ, axis=0, tiled=True) for s in shards[1:]]
    weights = [first] + later
    ids = group_ids()
    gain = norm_gain.reshape(layers * 8, 256)
    peers = lax.axis_size(SEQ)
    stream = hidden
    for l in range(layers):
        qf, kf, v, state = project(l, ids, gathered(stream), gain, weights[l], projection)
        slices = lax.all_to_all(state.reshape(peers, 256 // peers, 256), SEQ, 0, 0, tiled=True)
        num, den = local_attention(qf, kf, v)
        before = lax.all_to_all(prefix(slices), SEQ, 0, 0, tiled=True).reshape(256, 256)
        outs = finish(l, ids, qf, num, den, before, out_gain, weights[l])
        stream = (stream.astype(f32) + scattered(outs)).astype(bf16)
    return stream


def solution(mesh):
    finer = Mesh(mesh.devices.reshape(4, 8, X, 2), ("y", "z", "x", "c"))
    in_specs = (
        P(SEQ, GRP),
        P(None, SEQ, GRP),
        P(None, GRP, SEQ),
        P(None, GRP, None, None),
        P(),
        P(None, GRP),
    )
    return jax.shard_map(local, mesh=finer, in_specs=in_specs, out_specs=P(SEQ, GRP), check_vma=False)
```

```python
import jax
import jax.numpy as jnp
from jax import lax
from jax.experimental import pallas as pl
from jax.experimental.pallas import tpu as pltpu
from jax.sharding import Mesh
from jax.sharding import PartitionSpec as P

SEQ = ("y", "z")
GRP = ("x", "c")
X = 4
TILE = 256
STABILIZER = 2.0
bf16, f32 = jnp.bfloat16, jnp.float32
VMEM = pl.BlockSpec(memory_space=pltpu.VMEM)
SMEM = pl.BlockSpec(memory_space=pltpu.SMEM)
HBM = pl.BlockSpec(memory_space=pltpu.HBM)

SHIFTS = (0, 1, 3, 2)
SWAP = [(0, 1), (1, 0)]


def shifted(a, axis, by):
    n = lax.axis_size(axis)
    return lax.ppermute(a, axis, [(i, (i + by) % n) for i in range(n)]) if by else a


def swap(a):
    return lax.ppermute(a, "c", SWAP)


def group_ids():
    x, c = lax.axis_index("x"), lax.axis_index("c")
    came = [(x + X - s) % X * 2 + core for core in (c, 1 - c) for s in SHIFTS]
    goes = [(x + s) % X * 2 + core for core in (c, 1 - c) for s in SHIFTS]
    return jnp.stack(came + goes).astype(jnp.int32)


def dot(a, b, dims=((1,), (0,))):
    return lax.dot_general(a, b, (dims, ((), ())), preferred_element_type=f32)


def project_kernel(layer, ids, *refs):
    parts = refs[:8]
    gain, w_hbm, proj, qf_ref, kf_ref, v_ref, state_ref, w, scaled, squares, state, pair, low, sem = refs[8:]
    copies = []
    for k in range(8):
        rows = pl.ds(pl.multiple_of(ids[k] * 256, 256), 256)
        copies.append(
            pltpu.make_async_copy(w_hbm.at[rows, pl.ds(0, 768)], w.at[pl.ds(k * 256, 256)], sem.at[k])
        )
        copies[-1].start()
    for n in range(2):
        part = proj[layer, n] * 128 ** (-0.25)
        high = part.astype(bf16)
        rest = part - high.astype(f32)
        mid = rest.astype(bf16)
        pair[n, :, :128] = high
        pair[n, :, 128:] = mid
        low[n] = (rest - mid.astype(f32)).astype(bf16)
    tokens = parts[0].shape[0]
    gains = [gain[pl.ds(layer * 8 + ids[k], 1), :] for k in range(8)]
    state[...] = jnp.zeros_like(state)

    @pl.loop(0, tokens // 64)
    def _(i):
        rows = pl.ds(pl.multiple_of(i * 64, 64), 64)
        total = jnp.zeros((64, 256), f32)
        for k in range(8):
            wide = parts[k][rows, :].astype(f32)
            total += wide * wide
            scaled[rows, pl.ds(k * 256, 256)] = (wide * gains[k]).astype(bf16)
        squares[rows, :] = total[:, :128] + total[:, 128:]

    for copy in copies:
        copy.wait()
    ones = jnp.ones((TILE, 128), bf16)

    @pl.loop(0, tokens // TILE)
    def _(i):
        rows = pl.ds(pl.multiple_of(i * TILE, TILE), TILE)
        inverse_rms = lax.rsqrt(jnp.sum(squares[rows, :], axis=-1, keepdims=True) * (1.0 / 2048) + 1e-05)
        qkv = (dot(scaled[rows, :], w[...]) * inverse_rms).astype(bf16)
        for n in range(2):
            feats = []
            for j in range(2):
                u = qkv[:, n * 384 + j * 128 : n * 384 + (j + 1) * 128]
                both = dot(u, pair[n])
                mixed = both[:, :128] + (both[:, 128:] + dot(u, low[n]))
                uw = u.astype(f32)
                energy = jnp.sum(uw * uw, axis=-1, keepdims=True) * (0.5 * 128 ** (-0.5))
                feats.append((jnp.exp(mixed - energy - STABILIZER) * 128 ** (-0.5)).astype(bf16))
            value = qkv[:, n * 384 + 256 : n * 384 + 384]
            cols = pl.ds(n * 128, 128)
            qf_ref[rows, cols] = feats[0]
            kf_ref[rows, cols] = feats[1]
            v_ref[rows, cols] = value
            state[cols, :] += dot(feats[1], jnp.concatenate([value, ones], axis=1), ((0,), (0,)))

    state_ref[...] = state[...].astype(bf16)


def project(layer, ids, parts, gain, w, proj):
    tokens = parts[0].shape[0]
    half = jax.ShapeDtypeStruct((tokens, 256), bf16)
    return pl.pallas_call(
        lambda *refs: project_kernel(layer, *refs),
        name="project",
        out_shape=(half, half, half, jax.ShapeDtypeStruct((256, 256), bf16)),
        in_specs=[SMEM] + [VMEM] * 9 + [HBM, VMEM],
        out_specs=(VMEM,) * 4,
        scratch_shapes=[
            pltpu.VMEM((2048, 768), bf16),
            pltpu.VMEM((tokens, 2048), bf16),
            pltpu.VMEM((tokens, 128), f32),
            pltpu.VMEM((256, 256), f32),
            pltpu.VMEM((2, 128, 256), bf16),
            pltpu.VMEM((2, 128, 128), bf16),
            pltpu.SemaphoreType.DMA((8,)),
        ],
        cost_estimate=pl.CostEstimate(flops=2 * 512 * 2048 * 768, bytes_accessed=6 * 2**20, transcendentals=0),
        compiler_params=pltpu.CompilerParams(vmem_limit_bytes=48 * 2**20),
    )(ids, *parts, gain, w, proj)


def local_kernel(qf, kf, v, num_ref, den_ref):
    tile = 256
    keep = lax.broadcasted_iota(jnp.int32, (tile, tile), 0) >= lax.broadcasted_iota(jnp.int32, (tile, tile), 1)
    for n in range(2):
        cols = pl.ds(n * 128, 128)
        for i in range(qf.shape[0] // tile):
            rows = pl.ds(i * tile, tile)
            num = jnp.zeros((tile, 128), f32)
            den = jnp.zeros((tile, 1), f32)
            for j in range(i + 1):
                keys = pl.ds(j * tile, tile)
                scores = dot(qf[rows, cols], kf[keys, cols], ((1,), (1,)))
                if j == i:
                    scores = jnp.where(keep, scores, 0.0)
                den += jnp.sum(scores, axis=-1, keepdims=True)
                num += dot(scores.astype(bf16), v[keys, cols])
            num_ref[rows, cols] = num
            den_ref[rows, cols] = jnp.broadcast_to(den, (tile, 128))


def local_attention(qf, kf, v):
    whole = jax.ShapeDtypeStruct(qf.shape, f32)
    return pl.pallas_call(
        local_kernel,
        name="local_attention",
        out_shape=(whole, whole),
        in_specs=[VMEM] * 3,
        out_specs=(VMEM,) * 2,
        cost_estimate=pl.CostEstimate(flops=2 * 4 * 512 * 512 * 128, bytes_accessed=2 * 2**20, transcendentals=0),
        compiler_params=pltpu.CompilerParams(vmem_limit_bytes=48 * 2**20),
    )(qf, kf, v)


def prefix_kernel(peers, in_ref, out_ref):
    n = in_ref.shape[0]
    width = n // peers
    row = lax.broadcasted_iota(jnp.int32, (n, n), 0)
    col = lax.broadcasted_iota(jnp.int32, (n, n), 1)
    earlier = (col < row // width * width) & (row % width == col % width)
    out_ref[...] = dot(earlier.astype(f32).astype(bf16), in_ref[...]).astype(bf16)


def prefix(slices, peers):
    return pl.pallas_call(
        lambda *refs: prefix_kernel(peers, *refs),
        name="prefix",
        out_shape=jax.ShapeDtypeStruct(slices.shape, bf16),
        in_specs=[VMEM],
        out_specs=VMEM,
    )(slices)


def finish_kernel(layer, ids, qf, num, den, before, gain, w_hbm, *refs):
    outs = refs[:8]
    w, attended, sem = refs[8:]
    copies = []
    for k in range(8):
        rows = pl.ds(pl.multiple_of(ids[8 + k] * 256, 256), 256)
        copies.append(
            pltpu.make_async_copy(w_hbm.at[rows, pl.ds(768, 256)], w.at[pl.ds(k * 256, 256)], sem.at[k])
        )
        copies[-1].start()

    for n in range(2):
        cols = pl.ds(n * 128, 128)
        both = dot(qf[:, cols], before[cols, :])
        attention = (num[:, cols] + both[:, :128]) / (den[:, cols] + both[:, 128:])
        inverse = lax.rsqrt(jnp.sum(attention * attention, axis=-1, keepdims=True) * (1.0 / 128) + 1e-06)
        attended[:, cols] = (attention * inverse * gain[pl.ds(layer, 1), cols]).astype(bf16)
    for k in range(8):
        copies[k].wait()
        outs[k][...] = dot(attended[...], w[pl.ds(k * 256, 256), :], ((1,), (1,))).astype(bf16)


def finish(layer, ids, qf, num, den, before, gain, w):
    part = jax.ShapeDtypeStruct(qf.shape, bf16)
    return pl.pallas_call(
        lambda *refs: finish_kernel(layer, *refs),
        name="finish",
        out_shape=(part,) * 8,
        in_specs=[SMEM] + [VMEM] * 5 + [HBM],
        out_specs=(VMEM,) * 8,
        scratch_shapes=[pltpu.VMEM((2048, 256), bf16), pltpu.VMEM(qf.shape, bf16), pltpu.SemaphoreType.DMA((8,))],
        cost_estimate=pl.CostEstimate(flops=2 * 512 * 256 * 2304, bytes_accessed=5 * 2**20, transcendentals=0),
        compiler_params=pltpu.CompilerParams(vmem_limit_bytes=48 * 2**20),
    )(ids, qf, num, den, before, gain, w)


def gathered(own):
    mine = [shifted(own, "x", s) for s in SHIFTS]
    return mine + [swap(p) for p in mine]


def scattered(outs):
    sums = [m.astype(f32) + swap(o).astype(f32) for m, o in zip(outs[:4], outs[4:])]
    return sums[0] + sum(shifted(a.astype(bf16), "x", s).astype(f32) for a, s in zip(sums[1:], SHIFTS[1:]))


def local(hidden, qkv_weight, out_weight, projection, norm_gain, out_gain):
    layers = qkv_weight.shape[0]
    out_t = jnp.swapaxes(out_weight, 1, 2)
    shards = [jnp.concatenate([qkv_weight[l], out_t[l]], axis=1) for l in range(layers)]
    first = lax.all_gather(shards[0], SEQ, axis=0, tiled=True)
    later = [lax.all_gather(s, SEQ, axis=0, tiled=True) for s in shards[1:]]
    weights = [first] + later
    ids = group_ids()
    gain = norm_gain.reshape(layers * 8, 256)
    peers = lax.axis_size(SEQ)
    stream = hidden
    for l in range(layers):
        qf, kf, v, state = project(l, ids, gathered(stream), gain, weights[l], projection)
        slices = lax.all_to_all(state.reshape(peers, 256 // peers, 256), SEQ, 0, 0, tiled=True).reshape(256, 256)
        num, den = local_attention(qf, kf, v)
        sums = prefix(slices, peers).reshape(peers, 256 // peers, 256)
        before = lax.all_to_all(sums, SEQ, 0, 0, tiled=True).reshape(256, 256)
        outs = finish(l, ids, qf, num, den, before, out_gain, weights[l])
        stream = (stream.astype(f32) + scattered(outs)).astype(bf16)
    return stream


def solution(mesh):
    finer = Mesh(mesh.devices.reshape(4, 8, X, 2), ("y", "z", "x", "c"))
    in_specs = (
        P(SEQ, GRP),
        P(None, SEQ, GRP),
        P(None, GRP, SEQ),
        P(None, GRP, None, None),
        P(),
        P(None, GRP),
    )
    return jax.shard_map(local, mesh=finer, in_specs=in_specs, out_specs=P(SEQ, GRP), check_vma=False)
```

```python
import jax
import jax.numpy as jnp
from jax import lax
from jax.experimental import pallas as pl
from jax.experimental.pallas import tpu as pltpu
from jax.sharding import Mesh
from jax.sharding import PartitionSpec as P

SEQ = ("y", "z")
GRP = ("x", "c")
X = 4
TILE = 256
STABILIZER = 2.0
bf16, f32 = jnp.bfloat16, jnp.float32
VMEM = pl.BlockSpec(memory_space=pltpu.VMEM)
SMEM = pl.BlockSpec(memory_space=pltpu.SMEM)
HBM = pl.BlockSpec(memory_space=pltpu.HBM)

SHIFTS = (0, 1, 3, 2)
SHIFTS8 = (0, 1, 7, 2, 6, 3, 5, 4)
SWAP = [(0, 1), (1, 0)]


def shifted(a, axis, by):
    n = lax.axis_size(axis)
    return lax.ppermute(a, axis, [(i, (i + by) % n) for i in range(n)]) if by else a


def swap(a):
    return lax.ppermute(a, "c", SWAP)


def group_ids():
    x, c = lax.axis_index("x"), lax.axis_index("c")
    came = [(x + X - s) % X * 2 + core for core in (c, 1 - c) for s in SHIFTS]
    goes = [(x + s) % X * 2 + core for core in (c, 1 - c) for s in SHIFTS]
    return jnp.stack(came + goes + [lax.axis_index("y"), lax.axis_index("z")]).astype(jnp.int32)


def dot(a, b, dims=((1,), (0,))):
    return lax.dot_general(a, b, (dims, ((), ())), preferred_element_type=f32)


def load_weights(ids, refs, w, first, sem):
    width = w.shape[1]
    if len(refs) == 1:
        copy = pltpu.make_async_copy(refs[0].at[:, pl.ds(first, width)], w, sem.at[0])
        copy.start()
        return [copy]
    copies = []
    for ref, rows, column, dy, dz in PIECES:
        low, high = max(column, first), min(column + 512, first + width)
        if low < high:
            at = ((ids[16] + 4 - dy) % 4 * 8 + (ids[17] + 8 - dz) % 8) * 64
            copy = pltpu.make_async_copy(
                refs[ref].at[pl.ds(rows, 64), pl.ds(low - column, high - low)],
                w.at[pl.ds(pl.multiple_of(at, 64), 64), pl.ds(low - first, high - low)],
                sem.at[len(copies)],
            )
            copy.start()
            copies.append(copy)
    return copies


def pieces():
    table = []
    for i, dz in enumerate((0, 1, 7, 2, 6, 3, 5)):
        table += [(i, 64 * j, 0, dy, dz) for j, dy in enumerate(SHIFTS)]
    table += [(7 + j // 2, 64 * (j % 2), 0, dy, 4) for j, dy in enumerate(SHIFTS)]
    for i, dy in enumerate(SHIFTS):
        table += [(9 + i, 64 * j, 512, dy, dz) for j, dz in enumerate(SHIFTS8)]
    return table


PIECES = pieces()


def weights_by_permutes(shard):
    low, high = shard[:, :512], shard[:, 512:]
    column = jnp.concatenate([shifted(low, "y", s) for s in SHIFTS], axis=0)
    row = jnp.concatenate([shifted(high, "z", s) for s in SHIFTS8], axis=0)
    relayed = [column]
    up = down = column
    for _ in range(3):
        up, down = shifted(up, "z", 1), shifted(down, "z", 7)
        relayed += [up, down]
    relayed += [shifted(up[:128], "z", 1), shifted(down[128:], "z", 7)]
    return relayed + [shifted(row, "y", s) for s in SHIFTS]


def project_kernel(layer, ids, *refs):
    parts, refs = refs[:8], refs[8:]
    weights, refs = refs[:-13], refs[-13:]
    gain, proj, qf_ref, kf_ref, v_ref, state_ref, w, scaled, squares, state, pair, low, sem = refs
    copies = load_weights(ids, weights, w, 0, sem)
    for n in range(2):
        part = proj[layer, n] * 128 ** (-0.25)
        high = part.astype(bf16)
        rest = part - high.astype(f32)
        mid = rest.astype(bf16)
        pair[n, :, :128] = high
        pair[n, :, 128:] = mid
        low[n] = (rest - mid.astype(f32)).astype(bf16)
    tokens = parts[0].shape[0]
    gains = [gain[pl.ds(layer * 8 + ids[k], 1), :] for k in range(8)]
    state[...] = jnp.zeros_like(state)

    @pl.loop(0, tokens // 64)
    def _(i):
        rows = pl.ds(pl.multiple_of(i * 64, 64), 64)
        total = jnp.zeros((64, 256), f32)
        for k in range(8):
            wide = parts[k][rows, :].astype(f32)
            total += wide * wide
            scaled[rows, pl.ds(pl.multiple_of(ids[k] * 256, 256), 256)] = (wide * gains[k]).astype(bf16)
        squares[rows, :] = total[:, :128] + total[:, 128:]

    for copy in copies:
        copy.wait()
    ones = jnp.ones((TILE, 128), bf16)

    @pl.loop(0, tokens // TILE)
    def _(i):
        rows = pl.ds(pl.multiple_of(i * TILE, TILE), TILE)
        inverse_rms = lax.rsqrt(jnp.sum(squares[rows, :], axis=-1, keepdims=True) * (1.0 / 2048) + 1e-05)
        qkv = (dot(scaled[rows, :], w[...]) * inverse_rms).astype(bf16)
        for n in range(2):
            feats = []
            for j in range(2):
                u = qkv[:, n * 384 + j * 128 : n * 384 + (j + 1) * 128]
                both = dot(u, pair[n])
                mixed = both[:, :128] + (both[:, 128:] + dot(u, low[n]))
                uw = u.astype(f32)
                energy = jnp.sum(uw * uw, axis=-1, keepdims=True) * (0.5 * 128 ** (-0.5))
                feats.append((jnp.exp(mixed - energy - STABILIZER) * 128 ** (-0.5)).astype(bf16))
            value = qkv[:, n * 384 + 256 : n * 384 + 384]
            cols = pl.ds(n * 128, 128)
            qf_ref[rows, cols] = feats[0]
            kf_ref[rows, cols] = feats[1]
            v_ref[rows, cols] = value
            state[cols, :] += dot(feats[1], jnp.concatenate([value, ones], axis=1), ((0,), (0,)))

    state_ref[...] = state[...].astype(bf16)


def project(layer, ids, parts, gain, w, proj):
    tokens = parts[0].shape[0]
    half = jax.ShapeDtypeStruct((tokens, 256), bf16)
    return pl.pallas_call(
        lambda *refs: project_kernel(layer, *refs),
        name="project",
        out_shape=(half, half, half, jax.ShapeDtypeStruct((256, 256), bf16)),
        in_specs=[SMEM] + [VMEM] * 8 + [HBM] * len(w) + [VMEM] * 2,
        out_specs=(VMEM,) * 4,
        scratch_shapes=[
            pltpu.VMEM((2048, 768), bf16),
            pltpu.VMEM((tokens, 2048), bf16),
            pltpu.VMEM((tokens, 128), f32),
            pltpu.VMEM((256, 256), f32),
            pltpu.VMEM((2, 128, 256), bf16),
            pltpu.VMEM((2, 128, 128), bf16),
            pltpu.SemaphoreType.DMA((64,)),
        ],
        cost_estimate=pl.CostEstimate(flops=2 * 512 * 2048 * 768, bytes_accessed=6 * 2**20, transcendentals=0),
        compiler_params=pltpu.CompilerParams(vmem_limit_bytes=(48 if len(w) == 1 else 16) * 2**20),
    )(ids, *parts, *w, gain, proj)


def local_kernel(qf, kf, v, num_ref, den_ref):
    tile = 256
    keep = lax.broadcasted_iota(jnp.int32, (tile, tile), 0) >= lax.broadcasted_iota(jnp.int32, (tile, tile), 1)
    for n in range(2):
        cols = pl.ds(n * 128, 128)
        for i in range(qf.shape[0] // tile):
            rows = pl.ds(i * tile, tile)
            num = jnp.zeros((tile, 128), f32)
            den = jnp.zeros((tile, 1), f32)
            for j in range(i + 1):
                keys = pl.ds(j * tile, tile)
                scores = dot(qf[rows, cols], kf[keys, cols], ((1,), (1,)))
                if j == i:
                    scores = jnp.where(keep, scores, 0.0)
                den += jnp.sum(scores, axis=-1, keepdims=True)
                num += dot(scores.astype(bf16), v[keys, cols])
            num_ref[rows, cols] = num
            den_ref[rows, cols] = jnp.broadcast_to(den, (tile, 128))


def local_attention(qf, kf, v):
    whole = jax.ShapeDtypeStruct(qf.shape, f32)
    return pl.pallas_call(
        local_kernel,
        name="local_attention",
        out_shape=(whole, whole),
        in_specs=[VMEM] * 3,
        out_specs=(VMEM,) * 2,
        cost_estimate=pl.CostEstimate(flops=2 * 4 * 512 * 512 * 128, bytes_accessed=2 * 2**20, transcendentals=0),
        compiler_params=pltpu.CompilerParams(vmem_limit_bytes=16 * 2**20),
    )(qf, kf, v)


def prefix_kernel(peers, in_ref, out_ref):
    n = in_ref.shape[0]
    width = n // peers
    row = lax.broadcasted_iota(jnp.int32, (n, n), 0)
    col = lax.broadcasted_iota(jnp.int32, (n, n), 1)
    earlier = (col < (row & -width)) & (((row ^ col) & (width - 1)) == 0)
    out_ref[...] = dot(earlier.astype(f32).astype(bf16), in_ref[...]).astype(bf16)


def prefix(slices, peers):
    return pl.pallas_call(
        lambda *refs: prefix_kernel(peers, *refs),
        name="prefix",
        out_shape=jax.ShapeDtypeStruct(slices.shape, bf16),
        in_specs=[VMEM],
        out_specs=VMEM,
    )(slices)


def finish_kernel(layer, ids, qf, num, den, before, gain, *refs):
    weights, outs = refs[:-11], refs[-11:-3]
    w, attended, sem = refs[-3:]
    copies = load_weights(ids, weights, w, 768, sem)

    for n in range(2):
        cols = pl.ds(n * 128, 128)
        both = dot(qf[:, cols], before[cols, :])
        attention = (num[:, cols] + both[:, :128]) / (den[:, cols] + both[:, 128:])
        inverse = lax.rsqrt(jnp.sum(attention * attention, axis=-1, keepdims=True) * (1.0 / 128) + 1e-06)
        attended[:, cols] = (attention * inverse * gain[pl.ds(layer, 1), cols]).astype(bf16)
    for copy in copies:
        copy.wait()
    for k in range(8):
        rows = pl.ds(pl.multiple_of(ids[8 + k] * 256, 256), 256)
        outs[k][...] = dot(attended[...], w[rows, :], ((1,), (1,))).astype(bf16)


def finish(layer, ids, qf, num, den, before, gain, w):
    part = jax.ShapeDtypeStruct(qf.shape, bf16)
    return pl.pallas_call(
        lambda *refs: finish_kernel(layer, *refs),
        name="finish",
        out_shape=(part,) * 8,
        in_specs=[SMEM] + [VMEM] * 5 + [HBM] * len(w),
        out_specs=(VMEM,) * 8,
        scratch_shapes=[pltpu.VMEM((2048, 256), bf16), pltpu.VMEM(qf.shape, bf16), pltpu.SemaphoreType.DMA((32,))],
        cost_estimate=pl.CostEstimate(flops=2 * 512 * 256 * 2304, bytes_accessed=5 * 2**20, transcendentals=0),
        compiler_params=pltpu.CompilerParams(vmem_limit_bytes=(48 if len(w) == 1 else 16) * 2**20),
    )(ids, qf, num, den, before, gain, *w)


def gathered(own):
    mine = [shifted(own, "x", s) for s in SHIFTS]
    return mine + [swap(p) for p in mine]


def scattered(outs):
    sums = [m.astype(f32) + swap(o).astype(f32) for m, o in zip(outs[:4], outs[4:])]
    return sums[0] + sum(shifted(a.astype(bf16), "x", s).astype(f32) for a, s in zip(sums[1:], SHIFTS[1:]))


def local(hidden, qkv_weight, out_weight, projection, norm_gain, out_gain):
    layers = qkv_weight.shape[0]
    out_t = jnp.swapaxes(out_weight, 1, 2)
    shards = [jnp.concatenate([qkv_weight[l], out_t[l]], axis=1) for l in range(layers)]
    weights = [weights_by_permutes(shards[0])]
    weights += [[lax.all_gather(s, SEQ, axis=0, tiled=True)] for s in shards[1:]]
    ids = group_ids()
    gain = norm_gain.reshape(layers * 8, 256)
    peers = lax.axis_size(SEQ)
    stream = hidden
    for l in range(layers):
        qf, kf, v, state = project(l, ids, gathered(stream), gain, weights[l], projection)
        slices = lax.all_to_all(state.reshape(peers, 256 // peers, 256), SEQ, 0, 0, tiled=True).reshape(256, 256)
        num, den = local_attention(qf, kf, v)
        sums = prefix(slices, peers).reshape(peers, 256 // peers, 256)
        before = lax.all_to_all(sums, SEQ, 0, 0, tiled=True).reshape(256, 256)
        outs = finish(l, ids, qf, num, den, before, out_gain, weights[l])
        stream = (stream.astype(f32) + scattered(outs)).astype(bf16)
    return stream


def solution(mesh):
    finer = Mesh(mesh.devices.reshape(4, 8, X, 2), ("y", "z", "x", "c"))
    in_specs = (
        P(SEQ, GRP),
        P(None, SEQ, GRP),
        P(None, GRP, SEQ),
        P(None, GRP, None, None),
        P(),
        P(None, GRP),
    )
    return jax.shard_map(local, mesh=finer, in_specs=in_specs, out_specs=P(SEQ, GRP), check_vma=False)
```

```python
import jax
import jax.numpy as jnp
from jax import lax
from jax.experimental import pallas as pl
from jax.experimental.pallas import tpu as pltpu
from jax.sharding import Mesh
from jax.sharding import PartitionSpec as P

SEQ = ("y", "z")
GRP = ("x", "c")
X = 4
TILE = 256
STABILIZER = 2.0
bf16, f32 = jnp.bfloat16, jnp.float32
VMEM = pl.BlockSpec(memory_space=pltpu.VMEM)
SMEM = pl.BlockSpec(memory_space=pltpu.SMEM)
HBM = pl.BlockSpec(memory_space=pltpu.HBM)

SHIFTS = (0, 1, 3, 2)
SWAP = [(0, 1), (1, 0)]


def shifted(a, axis, by):
    n = lax.axis_size(axis)
    return lax.ppermute(a, axis, [(i, (i + by) % n) for i in range(n)]) if by else a


def swap(a):
    return lax.ppermute(a, "c", SWAP)


def group_ids():
    x, c = lax.axis_index("x"), lax.axis_index("c")
    came = [(x + X - s) % X * 2 + core for core in (c, 1 - c) for s in SHIFTS]
    goes = [(x + s) % X * 2 + core for core in (c, 1 - c) for s in SHIFTS]
    return jnp.stack(came + goes + [lax.axis_index("y"), lax.axis_index("z")]).astype(jnp.int32)


def dot(a, b, dims=((1,), (0,))):
    return lax.dot_general(a, b, (dims, ((), ())), preferred_element_type=f32)


def load_weights(ids, weights, w, first, sem):
    copies = []
    for i, dy in enumerate(SHIFTS):
        copy = pltpu.make_async_copy(
            weights.at[:, i, :, pl.ds(first, w.shape[-1])], w.at[(ids[16] + 4 - dy) % 4], sem.at[i]
        )
        copy.start()
        copies.append(copy)
    return copies


def weights_by_layer(shards):
    first = jnp.concatenate([shifted(shards[0], "y", s) for s in SHIFTS], axis=0)
    held, first = lax.optimization_barrier((jnp.concatenate(shards[1:], axis=0), first))
    later = [shifted(held, "y", s) for s in SHIFTS]
    columns = [first]
    for l in range(len(shards) - 1):
        columns.append(jnp.concatenate([p[64 * l : 64 * (l + 1)] for p in later], axis=0))
    return [lax.all_gather(c, "z", axis=0, tiled=True).reshape(8, 4, 64, 1024) for c in columns]


def project_kernel(layer, ids, *refs):
    parts, weights, refs = refs[:8], refs[8], refs[9:]
    gain, proj, qf_ref, kf_ref, v_ref, state_ref, w, scaled, squares, state, pair, low, sem = refs
    copies = load_weights(ids, weights, w, 0, sem)
    for n in range(2):
        part = proj[layer, n] * 128 ** (-0.25)
        high = part.astype(bf16)
        rest = part - high.astype(f32)
        mid = rest.astype(bf16)
        pair[n, :, :128] = high
        pair[n, :, 128:] = mid
        low[n] = (rest - mid.astype(f32)).astype(bf16)
    tokens = parts[0].shape[0]
    gains = [gain[pl.ds(layer * 8 + ids[k], 1), :] for k in range(8)]
    state[...] = jnp.zeros_like(state)

    @pl.loop(0, tokens // 64)
    def _(i):
        rows = pl.ds(pl.multiple_of(i * 64, 64), 64)
        total = jnp.zeros((64, 256), f32)
        for k in range(8):
            wide = parts[k][rows, :].astype(f32)
            total += wide * wide
            scaled[rows, pl.ds(pl.multiple_of(ids[k] * 256, 256), 256)] = (wide * gains[k]).astype(bf16)
        squares[rows, :] = total[:, :128] + total[:, 128:]

    for copy in copies:
        copy.wait()
    ones = jnp.ones((TILE, 128), bf16)

    @pl.loop(0, tokens // TILE)
    def _(i):
        rows = pl.ds(pl.multiple_of(i * TILE, TILE), TILE)
        inverse_rms = lax.rsqrt(jnp.sum(squares[rows, :], axis=-1, keepdims=True) * (1.0 / 2048) + 1e-05)
        qkv = (dot(scaled[rows, :], w[...].reshape(2048, 768)) * inverse_rms).astype(bf16)
        for n in range(2):
            feats = []
            for j in range(2):
                u = qkv[:, n * 384 + j * 128 : n * 384 + (j + 1) * 128]
                both = dot(u, pair[n])
                mixed = both[:, :128] + (both[:, 128:] + dot(u, low[n]))
                uw = u.astype(f32)
                energy = jnp.sum(uw * uw, axis=-1, keepdims=True) * (0.5 * 128 ** (-0.5))
                feats.append((jnp.exp(mixed - energy - STABILIZER) * 128 ** (-0.5)).astype(bf16))
            value = qkv[:, n * 384 + 256 : n * 384 + 384]
            cols = pl.ds(n * 128, 128)
            qf_ref[rows, cols] = feats[0]
            kf_ref[rows, cols] = feats[1]
            v_ref[rows, cols] = value
            state[cols, :] += dot(feats[1], jnp.concatenate([value, ones], axis=1), ((0,), (0,)))

    state_ref[...] = state[...].astype(bf16)


def project(layer, ids, parts, gain, w, proj):
    tokens = parts[0].shape[0]
    half = jax.ShapeDtypeStruct((tokens, 256), bf16)
    return pl.pallas_call(
        lambda *refs: project_kernel(layer, *refs),
        name="project",
        out_shape=(half, half, half, jax.ShapeDtypeStruct((256, 256), bf16)),
        in_specs=[SMEM] + [VMEM] * 8 + [HBM] + [VMEM] * 2,
        out_specs=(VMEM,) * 4,
        scratch_shapes=[
            pltpu.VMEM((4, 8, 64, 768), bf16),
            pltpu.VMEM((tokens, 2048), bf16),
            pltpu.VMEM((tokens, 128), f32),
            pltpu.VMEM((256, 256), f32),
            pltpu.VMEM((2, 128, 256), bf16),
            pltpu.VMEM((2, 128, 128), bf16),
            pltpu.SemaphoreType.DMA((4,)),
        ],
        cost_estimate=pl.CostEstimate(flops=2 * 512 * 2048 * 768, bytes_accessed=6 * 2**20, transcendentals=0),
        compiler_params=pltpu.CompilerParams(vmem_limit_bytes=48 * 2**20),
    )(ids, *parts, w, gain, proj)


def local_kernel(qf, kf, v, num_ref, den_ref):
    tile = 256
    keep = lax.broadcasted_iota(jnp.int32, (tile, tile), 0) >= lax.broadcasted_iota(jnp.int32, (tile, tile), 1)
    for n in range(2):
        cols = pl.ds(n * 128, 128)
        for i in range(qf.shape[0] // tile):
            rows = pl.ds(i * tile, tile)
            num = jnp.zeros((tile, 128), f32)
            den = jnp.zeros((tile, 1), f32)
            for j in range(i + 1):
                keys = pl.ds(j * tile, tile)
                scores = dot(qf[rows, cols], kf[keys, cols], ((1,), (1,)))
                if j == i:
                    scores = jnp.where(keep, scores, 0.0)
                den += jnp.sum(scores, axis=-1, keepdims=True)
                num += dot(scores.astype(bf16), v[keys, cols])
            num_ref[rows, cols] = num
            den_ref[rows, cols] = jnp.broadcast_to(den, (tile, 128))


def local_attention(qf, kf, v):
    whole = jax.ShapeDtypeStruct(qf.shape, f32)
    return pl.pallas_call(
        local_kernel,
        name="local_attention",
        out_shape=(whole, whole),
        in_specs=[VMEM] * 3,
        out_specs=(VMEM,) * 2,
        cost_estimate=pl.CostEstimate(flops=2 * 4 * 512 * 512 * 128, bytes_accessed=2 * 2**20, transcendentals=0),
        compiler_params=pltpu.CompilerParams(vmem_limit_bytes=16 * 2**20),
    )(qf, kf, v)


def prefix_kernel(peers, in_ref, out_ref):
    n = in_ref.shape[0]
    width = n // peers
    row = lax.broadcasted_iota(jnp.int32, (n, n), 0)
    col = lax.broadcasted_iota(jnp.int32, (n, n), 1)
    earlier = (col < (row & -width)) & (((row ^ col) & (width - 1)) == 0)
    out_ref[...] = dot(earlier.astype(f32).astype(bf16), in_ref[...]).astype(bf16)


def prefix(slices, peers):
    return pl.pallas_call(
        lambda *refs: prefix_kernel(peers, *refs),
        name="prefix",
        out_shape=jax.ShapeDtypeStruct(slices.shape, bf16),
        in_specs=[VMEM],
        out_specs=VMEM,
    )(slices)


def finish_kernel(layer, ids, qf, num, den, before, gain, *refs):
    weights, outs = refs[0], refs[1:9]
    w, attended, sem = refs[-3:]
    copies = load_weights(ids, weights, w, 768, sem)

    for n in range(2):
        cols = pl.ds(n * 128, 128)
        both = dot(qf[:, cols], before[cols, :])
        attention = (num[:, cols] + both[:, :128]) / (den[:, cols] + both[:, 128:])
        inverse = lax.rsqrt(jnp.sum(attention * attention, axis=-1, keepdims=True) * (1.0 / 128) + 1e-06)
        attended[:, cols] = (attention * inverse * gain[pl.ds(layer, 1), cols]).astype(bf16)
    for copy in copies:
        copy.wait()
    for k in range(8):
        group = ids[8 + k]
        part = w[group // 2, pl.ds(group % 2 * 4, 4)].reshape(256, 256)
        outs[k][...] = dot(attended[...], part, ((1,), (1,))).astype(bf16)


def finish(layer, ids, qf, num, den, before, gain, w):
    part = jax.ShapeDtypeStruct(qf.shape, bf16)
    return pl.pallas_call(
        lambda *refs: finish_kernel(layer, *refs),
        name="finish",
        out_shape=(part,) * 8,
        in_specs=[SMEM] + [VMEM] * 5 + [HBM],
        out_specs=(VMEM,) * 8,
        scratch_shapes=[pltpu.VMEM((4, 8, 64, 256), bf16), pltpu.VMEM(qf.shape, bf16), pltpu.SemaphoreType.DMA((4,))],
        cost_estimate=pl.CostEstimate(flops=2 * 512 * 256 * 2304, bytes_accessed=5 * 2**20, transcendentals=0),
        compiler_params=pltpu.CompilerParams(vmem_limit_bytes=48 * 2**20),
    )(ids, qf, num, den, before, gain, w)


def gathered(own):
    mine = [shifted(own, "x", s) for s in SHIFTS]
    return mine + [swap(p) for p in mine]


def scattered(outs):
    sums = [m.astype(f32) + swap(o).astype(f32) for m, o in zip(outs[:4], outs[4:])]
    return sums[0] + sum(shifted(a.astype(bf16), "x", s).astype(f32) for a, s in zip(sums[1:], SHIFTS[1:]))


def local(hidden, qkv_weight, out_weight, projection, norm_gain, out_gain):
    layers = qkv_weight.shape[0]
    out_t = jnp.swapaxes(out_weight, 1, 2)
    shards = [jnp.concatenate([qkv_weight[l], out_t[l]], axis=1) for l in range(layers)]
    weights = weights_by_layer(shards)
    ids = group_ids()
    gain = norm_gain.reshape(layers * 8, 256)
    peers = lax.axis_size(SEQ)
    stream = hidden
    for l in range(layers):
        qf, kf, v, state = project(l, ids, gathered(stream), gain, weights[l], projection)
        slices = lax.all_to_all(state.reshape(peers, 256 // peers, 256), SEQ, 0, 0, tiled=True).reshape(256, 256)
        num, den = local_attention(qf, kf, v)
        sums = prefix(slices, peers).reshape(peers, 256 // peers, 256)
        before = lax.all_to_all(sums, SEQ, 0, 0, tiled=True).reshape(256, 256)
        outs = finish(l, ids, qf, num, den, before, out_gain, weights[l])
        stream = (stream.astype(f32) + scattered(outs)).astype(bf16)
    return stream


def solution(mesh):
    finer = Mesh(mesh.devices.reshape(4, 8, X, 2), ("y", "z", "x", "c"))
    in_specs = (
        P(SEQ, GRP),
        P(None, SEQ, GRP),
        P(None, GRP, SEQ),
        P(None, GRP, None, None),
        P(),
        P(None, GRP),
    )
    return jax.shard_map(local, mesh=finer, in_specs=in_specs, out_specs=P(SEQ, GRP), check_vma=False)
```

```python
import jax
import jax.numpy as jnp
from jax import lax
from jax.experimental import pallas as pl
from jax.experimental.pallas import tpu as pltpu
from jax.sharding import Mesh
from jax.sharding import PartitionSpec as P

SEQ = ("y", "z")
GRP = ("x", "c")
X = 4
TILE = 256
LIMIT = 50 * 2**20
STABILIZER = 2.0
bf16, f32 = jnp.bfloat16, jnp.float32
VMEM = pl.BlockSpec(memory_space=pltpu.VMEM)
SMEM = pl.BlockSpec(memory_space=pltpu.SMEM)
ANY = pl.BlockSpec(memory_space=pl.ANY)

SHIFTS = (0, 1, 3, 2)
SWAP = [(0, 1), (1, 0)]


def shifted(a, axis, by):
    n = lax.axis_size(axis)
    return lax.ppermute(a, axis, [(i, (i + by) % n) for i in range(n)]) if by else a


def swap(a):
    return lax.ppermute(a, "c", SWAP)


def group_ids():
    x, c = lax.axis_index("x"), lax.axis_index("c")
    came = [(x + X - s) % X * 2 + core for core in (c, 1 - c) for s in SHIFTS]
    goes = [(x + s) % X * 2 + core for core in (c, 1 - c) for s in SHIFTS]
    return jnp.stack(came + goes + [lax.axis_index("y"), lax.axis_index("z")]).astype(jnp.int32)


def dot(a, b, dims=((1,), (0,))):
    return lax.dot_general(a, b, (dims, ((), ())), preferred_element_type=f32)


def load_weights(ids, weights, w, first, sem):
    copies = []
    for ref, low, dz in RELAYED:
        for i in range(low, low + weights[ref].shape[0]):
            copy = pltpu.make_async_copy(
                weights[ref].at[i - low, :, pl.ds(first, w.shape[-1])],
                w.at[(ids[16] + 4 - SHIFTS[i]) % 4, (ids[17] + 8 - dz) % 8],
                sem.at[len(copies)],
            )
            copy.start()
            copies.append(copy)
    return copies


RELAYED = ((0, 0, 0), (1, 0, 1), (2, 0, 7), (3, 0, 2), (4, 0, 6), (5, 0, 3), (6, 0, 5), (7, 0, 4), (8, 2, 4))


def columns_of_weights(shards):
    first = jnp.stack([shifted(shards[0], "y", s) for s in SHIFTS])
    held, first = lax.optimization_barrier((jnp.concatenate(shards[1:], axis=0), first))
    later = [shifted(held, "y", s) for s in SHIFTS]
    return [first] + [jnp.stack([p[64 * l : 64 * (l + 1)] for p in later]) for l in range(len(shards) - 1)]


def relayed(column):
    up = down = column
    out = [column]
    for _ in range(3):
        up, down = shifted(up, "z", 1), shifted(down, "z", 7)
        out += [up, down]
    return out + [shifted(up[:2], "z", 1), shifted(down[2:], "z", 7)]


def project_kernel(layer, ids, *refs):
    parts, weights, refs = refs[:8], refs[8:17], refs[17:]
    gain, proj, qf_ref, kf_ref, v_ref, state_ref, w, scaled, squares, state, pair, low, sem = refs
    copies = load_weights(ids, weights, w, 0, sem)
    for n in range(2):
        part = proj[layer, n] * 128 ** (-0.25)
        high = part.astype(bf16)
        rest = part - high.astype(f32)
        mid = rest.astype(bf16)
        pair[n, :, :128] = high
        pair[n, :, 128:] = mid
        low[n] = (rest - mid.astype(f32)).astype(bf16)
    tokens = parts[0].shape[0]
    gains = [gain[pl.ds(layer * 8 + ids[k], 1), :] for k in range(8)]
    state[...] = jnp.zeros_like(state)

    @pl.loop(0, tokens // 64)
    def _(i):
        rows = pl.ds(pl.multiple_of(i * 64, 64), 64)
        total = jnp.zeros((64, 256), f32)
        for k in range(8):
            wide = parts[k][rows, :].astype(f32)
            total += wide * wide
            scaled[rows, pl.ds(pl.multiple_of(ids[k] * 256, 256), 256)] = (wide * gains[k]).astype(bf16)
        squares[rows, :] = total[:, :128] + total[:, 128:]

    for copy in copies:
        copy.wait()
    ones = jnp.ones((TILE, 128), bf16)

    @pl.loop(0, tokens // TILE)
    def _(i):
        rows = pl.ds(pl.multiple_of(i * TILE, TILE), TILE)
        inverse_rms = lax.rsqrt(jnp.sum(squares[rows, :], axis=-1, keepdims=True) * (1.0 / 2048) + 1e-05)
        qkv = (dot(scaled[rows, :], w[...].reshape(2048, 768)) * inverse_rms).astype(bf16)
        for n in range(2):
            feats = []
            for j in range(2):
                u = qkv[:, n * 384 + j * 128 : n * 384 + (j + 1) * 128]
                both = dot(u, pair[n])
                mixed = both[:, :128] + (both[:, 128:] + dot(u, low[n]))
                uw = u.astype(f32)
                energy = jnp.sum(uw * uw, axis=-1, keepdims=True) * (0.5 * 128 ** (-0.5))
                feats.append((jnp.exp(mixed - energy - STABILIZER) * 128 ** (-0.5)).astype(bf16))
            value = qkv[:, n * 384 + 256 : n * 384 + 384]
            cols = pl.ds(n * 128, 128)
            qf_ref[rows, cols] = feats[0]
            kf_ref[rows, cols] = feats[1]
            v_ref[rows, cols] = value
            state[cols, :] += dot(feats[1], jnp.concatenate([value, ones], axis=1), ((0,), (0,)))

    state_ref[...] = state[...].astype(bf16)


def project(layer, ids, parts, gain, w, proj):
    tokens = parts[0].shape[0]
    half = jax.ShapeDtypeStruct((tokens, 256), bf16)
    return pl.pallas_call(
        lambda *refs: project_kernel(layer, *refs),
        name="project",
        out_shape=(half, half, half, jax.ShapeDtypeStruct((256, 256), bf16)),
        in_specs=[SMEM] + [VMEM] * 8 + [ANY] * 9 + [VMEM] * 2,
        out_specs=(VMEM,) * 4,
        scratch_shapes=[
            pltpu.VMEM((4, 8, 64, 768), bf16),
            pltpu.VMEM((tokens, 2048), bf16),
            pltpu.VMEM((tokens, 128), f32),
            pltpu.VMEM((256, 256), f32),
            pltpu.VMEM((2, 128, 256), bf16),
            pltpu.VMEM((2, 128, 128), bf16),
            pltpu.SemaphoreType.DMA((32,)),
        ],
        cost_estimate=pl.CostEstimate(flops=2 * 512 * 2048 * 768, bytes_accessed=6 * 2**20, transcendentals=0),
        compiler_params=pltpu.CompilerParams(vmem_limit_bytes=LIMIT),
    )(ids, *parts, *w, gain, proj)


def local_kernel(qf, kf, v, num_ref, den_ref):
    tile = 256
    keep = lax.broadcasted_iota(jnp.int32, (tile, tile), 0) >= lax.broadcasted_iota(jnp.int32, (tile, tile), 1)
    for n in range(2):
        cols = pl.ds(n * 128, 128)
        for i in range(qf.shape[0] // tile):
            rows = pl.ds(i * tile, tile)
            num = jnp.zeros((tile, 128), f32)
            den = jnp.zeros((tile, 1), f32)
            for j in range(i + 1):
                keys = pl.ds(j * tile, tile)
                scores = dot(qf[rows, cols], kf[keys, cols], ((1,), (1,)))
                if j == i:
                    scores = jnp.where(keep, scores, 0.0)
                den += jnp.sum(scores, axis=-1, keepdims=True)
                num += dot(scores.astype(bf16), v[keys, cols])
            num_ref[rows, cols] = num
            den_ref[rows, cols] = jnp.broadcast_to(den, (tile, 128))


def local_attention(qf, kf, v):
    whole = jax.ShapeDtypeStruct(qf.shape, f32)
    return pl.pallas_call(
        local_kernel,
        name="local_attention",
        out_shape=(whole, whole),
        in_specs=[VMEM] * 3,
        out_specs=(VMEM,) * 2,
        cost_estimate=pl.CostEstimate(flops=2 * 4 * 512 * 512 * 128, bytes_accessed=2 * 2**20, transcendentals=0),
        compiler_params=pltpu.CompilerParams(vmem_limit_bytes=LIMIT),
    )(qf, kf, v)


def prefix_kernel(peers, in_ref, out_ref):
    n = in_ref.shape[0]
    width = n // peers
    row = lax.broadcasted_iota(jnp.int32, (n, n), 0)
    col = lax.broadcasted_iota(jnp.int32, (n, n), 1)
    earlier = (col < (row & -width)) & (((row ^ col) & (width - 1)) == 0)
    out_ref[...] = dot(earlier.astype(f32).astype(bf16), in_ref[...]).astype(bf16)


def prefix(slices, peers):
    return pl.pallas_call(
        lambda *refs: prefix_kernel(peers, *refs),
        name="prefix",
        out_shape=jax.ShapeDtypeStruct(slices.shape, bf16),
        in_specs=[VMEM],
        out_specs=VMEM,
        compiler_params=pltpu.CompilerParams(vmem_limit_bytes=LIMIT),
    )(slices)


def finish_kernel(layer, ids, qf, num, den, before, gain, *refs):
    weights, outs = refs[:9], refs[9:17]
    w, attended, sem = refs[-3:]
    copies = load_weights(ids, weights, w, 768, sem)

    for n in range(2):
        cols = pl.ds(n * 128, 128)
        both = dot(qf[:, cols], before[cols, :])
        attention = (num[:, cols] + both[:, :128]) / (den[:, cols] + both[:, 128:])
        inverse = lax.rsqrt(jnp.sum(attention * attention, axis=-1, keepdims=True) * (1.0 / 128) + 1e-06)
        attended[:, cols] = (attention * inverse * gain[pl.ds(layer, 1), cols]).astype(bf16)
    for copy in copies:
        copy.wait()
    for k in range(8):
        group = ids[8 + k]
        part = w[group // 2, pl.ds(group % 2 * 4, 4)].reshape(256, 256)
        outs[k][...] = dot(attended[...], part, ((1,), (1,))).astype(bf16)


def finish(layer, ids, qf, num, den, before, gain, w):
    part = jax.ShapeDtypeStruct(qf.shape, bf16)
    return pl.pallas_call(
        lambda *refs: finish_kernel(layer, *refs),
        name="finish",
        out_shape=(part,) * 8,
        in_specs=[SMEM] + [VMEM] * 5 + [ANY] * 9,
        out_specs=(VMEM,) * 8,
        scratch_shapes=[pltpu.VMEM((4, 8, 64, 256), bf16), pltpu.VMEM(qf.shape, bf16), pltpu.SemaphoreType.DMA((32,))],
        cost_estimate=pl.CostEstimate(flops=2 * 512 * 256 * 2304, bytes_accessed=5 * 2**20, transcendentals=0),
        compiler_params=pltpu.CompilerParams(vmem_limit_bytes=LIMIT),
    )(ids, qf, num, den, before, gain, *w)


def gathered(own):
    mine = [shifted(own, "x", s) for s in SHIFTS]
    return mine + [swap(p) for p in mine]


def scattered(outs):
    sums = [m.astype(f32) + swap(o).astype(f32) for m, o in zip(outs[:4], outs[4:])]
    return sums[0] + sum(shifted(a.astype(bf16), "x", s).astype(f32) for a, s in zip(sums[1:], SHIFTS[1:]))


def local(hidden, qkv_weight, out_weight, projection, norm_gain, out_gain):
    layers = qkv_weight.shape[0]
    out_t = jnp.swapaxes(out_weight, 1, 2)
    shards = [jnp.concatenate([qkv_weight[l], out_t[l]], axis=1) for l in range(layers)]
    columns = columns_of_weights(shards)
    weights = relayed(columns[0])
    ids = group_ids()
    gain = norm_gain.reshape(layers * 8, 256)
    peers = lax.axis_size(SEQ)
    stream = hidden
    for l in range(layers):
        qf, kf, v, state = project(l, ids, gathered(stream), gain, weights, projection)
        if l + 1 < layers:
            column, state = lax.optimization_barrier((columns[l + 1], state))
            coming = relayed(column)
        slices = lax.all_to_all(state.reshape(peers, 256 // peers, 256), SEQ, 0, 0, tiled=True).reshape(256, 256)
        num, den = local_attention(qf, kf, v)
        sums = prefix(slices, peers).reshape(peers, 256 // peers, 256)
        before = lax.all_to_all(sums, SEQ, 0, 0, tiled=True).reshape(256, 256)
        outs = finish(l, ids, qf, num, den, before, out_gain, weights)
        stream = (stream.astype(f32) + scattered(outs)).astype(bf16)
        weights = coming
    return stream


def solution(mesh):
    finer = Mesh(mesh.devices.reshape(4, 8, X, 2), ("y", "z", "x", "c"))
    in_specs = (
        P(SEQ, GRP),
        P(None, SEQ, GRP),
        P(None, GRP, SEQ),
        P(None, GRP, None, None),
        P(),
        P(None, GRP),
    )
    return jax.shard_map(local, mesh=finer, in_specs=in_specs, out_specs=P(SEQ, GRP), check_vma=False)
```

```python
import jax
import jax.numpy as jnp
from jax import lax
from jax.experimental import pallas as pl
from jax.experimental.pallas import tpu as pltpu
from jax.sharding import Mesh
from jax.sharding import PartitionSpec as P

SEQ = ("y", "z")
GRP = ("x", "c")
X = 4
TILE = 256
LIMIT = 50 * 2**20
STABILIZER = 2.0
bf16, f32 = jnp.bfloat16, jnp.float32
VMEM = pl.BlockSpec(memory_space=pltpu.VMEM)
SMEM = pl.BlockSpec(memory_space=pltpu.SMEM)
HBM = pl.BlockSpec(memory_space=pltpu.HBM)

SHIFTS = (0, 1, 3, 2)
SHIFTS8 = (0, 1, 7, 2, 6, 3, 5, 4)
SWAP = [(0, 1), (1, 0)]


def shifted(a, axis, by):
    n = lax.axis_size(axis)
    return lax.ppermute(a, axis, [(i, (i + by) % n) for i in range(n)]) if by else a


def swap(a):
    return lax.ppermute(a, "c", SWAP)


def group_ids():
    x, c = lax.axis_index("x"), lax.axis_index("c")
    came = [(x + X - s) % X * 2 + core for core in (c, 1 - c) for s in SHIFTS]
    goes = [(x + s) % X * 2 + core for core in (c, 1 - c) for s in SHIFTS]
    return jnp.stack(came + goes + [lax.axis_index("y"), lax.axis_index("z")]).astype(jnp.int32)


def dot(a, b, dims=((1,), (0,))):
    return lax.dot_general(a, b, (dims, ((), ())), preferred_element_type=f32)


def load_weights(ids, weights, w, first, at, width, sem):
    copies = []
    for i, dy in enumerate(SHIFTS):
        copy = pltpu.make_async_copy(
            weights.at[:, i, :, pl.ds(first, width)],
            w.at[(ids[16] + 4 - dy) % 4, :, :, pl.ds(at, width)],
            sem.at[i],
        )
        copy.start()
        copies.append(copy)
    return copies


def load_first_weights(ids, weights, w, sem):
    copies = []
    for i, dy in enumerate(SHIFTS):
        for j, dz in enumerate(SHIFTS8):
            copy = pltpu.make_async_copy(
                weights[i].at[j], w.at[(ids[16] + 4 - dy) % 4, (ids[17] + 8 - dz) % 8], sem.at[len(copies)]
            )
            copy.start()
            copies.append(copy)
    return copies


def gathered_over_z(column):
    whole = lax.all_gather(column.reshape(256, -1), "z", axis=0, tiled=True)
    return whole.reshape(8, 4, 64, -1)


def weights_by_layer(qkv_weight, out_t):
    first = jnp.stack([shifted(qkv_weight[0], "y", s) for s in SHIFTS])
    shards = [jnp.concatenate([qkv_weight[l], out_t[l]], axis=1) for l in range(1, qkv_weight.shape[0])]
    held, out, first = lax.optimization_barrier((jnp.concatenate(shards, axis=0), out_t[0], first))
    later = [shifted(held, "y", s) for s in SHIFTS]
    row = jnp.stack([shifted(out, "z", s) for s in SHIFTS8])
    weights = [gathered_over_z(first)]
    for l in range(len(shards)):
        weights.append(gathered_over_z(jnp.stack([p[64 * l : 64 * (l + 1)] for p in later])))
    return weights, [[shifted(row, "y", s) for s in SHIFTS]] + [[w] for w in weights[1:]]


def feature_tables(layer, proj, pair, low):
    for n in range(2):
        part = proj[layer, n] * 128 ** (-0.25)
        high = part.astype(bf16)
        rest = part - high.astype(f32)
        mid = rest.astype(bf16)
        pair[n, :, :128] = high
        pair[n, :, 128:] = mid
        low[n] = (rest - mid.astype(f32)).astype(bf16)


def features(u, pair, low):
    both = dot(u, pair)
    mixed = both[:, :128] + (both[:, 128:] + dot(u, low))
    uw = u.astype(f32)
    energy = jnp.sum(uw * uw, axis=-1, keepdims=True) * (0.5 * 128 ** (-0.5))
    return (jnp.exp(mixed - energy - STABILIZER) * 128 ** (-0.5)).astype(bf16)


def project_kernel(layer, ids, *refs):
    parts, weights, refs = refs[:8], refs[8], refs[9:]
    gain, proj, kf_ref, v_ref, state_ref, scaled, inverse_ref, w, squares, state, pair, low, sem = refs
    copies = []
    for n in range(2):
        copies += load_weights(ids, weights, w, n * 384 + 128, n * 256, 256, sem.at[n])
    feature_tables(layer, proj, pair, low)
    tokens = parts[0].shape[0]
    gains = [gain[pl.ds(layer * 8 + ids[k], 1), :] for k in range(8)]
    state[...] = jnp.zeros_like(state)

    @pl.loop(0, tokens // 64)
    def _(i):
        rows = pl.ds(pl.multiple_of(i * 64, 64), 64)
        total = jnp.zeros((64, 256), f32)
        for k in range(8):
            wide = parts[k][rows, :].astype(f32)
            total += wide * wide
            scaled[rows, pl.ds(pl.multiple_of(ids[k] * 256, 256), 256)] = (wide * gains[k]).astype(bf16)
        squares[rows, :] = total[:, :128] + total[:, 128:]

    for copy in copies:
        copy.wait()
    ones = jnp.ones((TILE, 128), bf16)

    @pl.loop(0, tokens // TILE)
    def _(i):
        rows = pl.ds(pl.multiple_of(i * TILE, TILE), TILE)
        inverse_rms = lax.rsqrt(jnp.sum(squares[rows, :], axis=-1, keepdims=True) * (1.0 / 2048) + 1e-05)
        inverse_ref[rows, :] = jnp.broadcast_to(inverse_rms, (TILE, 128))
        kv = (dot(scaled[rows, :], w[...].reshape(2048, 512)) * inverse_rms).astype(bf16)
        for n in range(2):
            key_feat = features(kv[:, n * 256 : n * 256 + 128], pair[n], low[n])
            value = kv[:, n * 256 + 128 : n * 256 + 256]
            cols = pl.ds(n * 128, 128)
            kf_ref[rows, cols] = key_feat
            v_ref[rows, cols] = value
            state[cols, :] += dot(key_feat, jnp.concatenate([value, ones], axis=1), ((0,), (0,)))

    state_ref[...] = state[...].astype(bf16)


def project(layer, ids, parts, gain, w, proj):
    tokens = parts[0].shape[0]
    half = jax.ShapeDtypeStruct((tokens, 256), bf16)
    return pl.pallas_call(
        lambda *refs: project_kernel(layer, *refs),
        name="project",
        out_shape=(
            half,
            half,
            jax.ShapeDtypeStruct((256, 256), bf16),
            jax.ShapeDtypeStruct((tokens, 2048), bf16),
            jax.ShapeDtypeStruct((tokens, 128), f32),
        ),
        in_specs=[SMEM] + [VMEM] * 8 + [HBM] + [VMEM] * 2,
        out_specs=(VMEM,) * 5,
        scratch_shapes=[
            pltpu.VMEM((4, 8, 64, 512), bf16),
            pltpu.VMEM((tokens, 128), f32),
            pltpu.VMEM((256, 256), f32),
            pltpu.VMEM((2, 128, 256), bf16),
            pltpu.VMEM((2, 128, 128), bf16),
            pltpu.SemaphoreType.DMA((2, 4)),
        ],
        cost_estimate=pl.CostEstimate(flops=2 * 512 * 2048 * 512, bytes_accessed=6 * 2**20, transcendentals=0),
        compiler_params=pltpu.CompilerParams(vmem_limit_bytes=LIMIT),
    )(ids, *parts, w, gain, proj)


def query_kernel(layer, ids, scaled, inverse, weights, proj, qf_ref, w, pair, low, sem):
    copies = []
    for n in range(2):
        copies += load_weights(ids, weights, w, n * 384, n * 128, 128, sem.at[n])
    feature_tables(layer, proj, pair, low)
    for copy in copies:
        copy.wait()

    @pl.loop(0, scaled.shape[0] // TILE)
    def _(i):
        rows = pl.ds(pl.multiple_of(i * TILE, TILE), TILE)
        query = dot(scaled[rows, :], w[...].reshape(2048, 256))
        for n in range(2):
            cols = pl.ds(n * 128, 128)
            u = (query[:, n * 128 : n * 128 + 128] * inverse[rows, :]).astype(bf16)
            qf_ref[rows, cols] = features(u, pair[n], low[n])


def queries(layer, ids, scaled, inverse, w, proj):
    return pl.pallas_call(
        lambda *refs: query_kernel(layer, *refs),
        name="queries",
        out_shape=jax.ShapeDtypeStruct((scaled.shape[0], 256), bf16),
        in_specs=[SMEM] + [VMEM] * 2 + [HBM, VMEM],
        out_specs=VMEM,
        scratch_shapes=[
            pltpu.VMEM((4, 8, 64, 256), bf16),
            pltpu.VMEM((2, 128, 256), bf16),
            pltpu.VMEM((2, 128, 128), bf16),
            pltpu.SemaphoreType.DMA((2, 4)),
        ],
        cost_estimate=pl.CostEstimate(flops=2 * 512 * 2048 * 256, bytes_accessed=4 * 2**20, transcendentals=0),
        compiler_params=pltpu.CompilerParams(vmem_limit_bytes=LIMIT),
    )(ids, scaled, inverse, w, proj)


def local_kernel(qf, kf, v, num_ref, den_ref):
    tile = 256
    keep = lax.broadcasted_iota(jnp.int32, (tile, tile), 0) >= lax.broadcasted_iota(jnp.int32, (tile, tile), 1)
    for n in range(2):
        cols = pl.ds(n * 128, 128)
        for i in range(qf.shape[0] // tile):
            rows = pl.ds(i * tile, tile)
            num = jnp.zeros((tile, 128), f32)
            den = jnp.zeros((tile, 1), f32)
            for j in range(i + 1):
                keys = pl.ds(j * tile, tile)
                scores = dot(qf[rows, cols], kf[keys, cols], ((1,), (1,)))
                if j == i:
                    scores = jnp.where(keep, scores, 0.0)
                den += jnp.sum(scores, axis=-1, keepdims=True)
                num += dot(scores.astype(bf16), v[keys, cols])
            num_ref[rows, cols] = num
            den_ref[rows, cols] = jnp.broadcast_to(den, (tile, 128))


def local_attention(qf, kf, v):
    whole = jax.ShapeDtypeStruct(qf.shape, f32)
    return pl.pallas_call(
        local_kernel,
        name="local_attention",
        out_shape=(whole, whole),
        in_specs=[VMEM] * 3,
        out_specs=(VMEM,) * 2,
        cost_estimate=pl.CostEstimate(flops=2 * 4 * 512 * 512 * 128, bytes_accessed=2 * 2**20, transcendentals=0),
        compiler_params=pltpu.CompilerParams(vmem_limit_bytes=LIMIT),
    )(qf, kf, v)


def prefix_kernel(peers, in_ref, out_ref):
    n = in_ref.shape[0]
    width = n // peers
    row = lax.broadcasted_iota(jnp.int32, (n, n), 0)
    col = lax.broadcasted_iota(jnp.int32, (n, n), 1)
    earlier = (col < (row & -width)) & (((row ^ col) & (width - 1)) == 0)
    out_ref[...] = dot(earlier.astype(f32).astype(bf16), in_ref[...]).astype(bf16)


def prefix(slices, peers):
    return pl.pallas_call(
        lambda *refs: prefix_kernel(peers, *refs),
        name="prefix",
        out_shape=jax.ShapeDtypeStruct(slices.shape, bf16),
        in_specs=[VMEM],
        out_specs=VMEM,
    )(slices)


def finish_kernel(layer, ids, qf, num, den, before, gain, *refs):
    weights, outs = refs[:-11], refs[-11:-3]
    w, attended, sem = refs[-3:]
    if len(weights) == 1:
        copies = load_weights(ids, weights[0], w, 768, 0, 256, sem)
    else:
        copies = load_first_weights(ids, weights, w, sem)

    for n in range(2):
        cols = pl.ds(n * 128, 128)
        both = dot(qf[:, cols], before[cols, :])
        attention = (num[:, cols] + both[:, :128]) / (den[:, cols] + both[:, 128:])
        inverse = lax.rsqrt(jnp.sum(attention * attention, axis=-1, keepdims=True) * (1.0 / 128) + 1e-06)
        attended[:, cols] = (attention * inverse * gain[pl.ds(layer, 1), cols]).astype(bf16)
    for copy in copies:
        copy.wait()
    for k in range(8):
        group = ids[8 + k]
        part = w[group // 2, pl.ds(group % 2 * 4, 4)].reshape(256, 256)
        outs[k][...] = dot(attended[...], part, ((1,), (1,))).astype(bf16)


def finish(layer, ids, qf, num, den, before, gain, w):
    part = jax.ShapeDtypeStruct(qf.shape, bf16)
    return pl.pallas_call(
        lambda *refs: finish_kernel(layer, *refs),
        name="finish",
        out_shape=(part,) * 8,
        in_specs=[SMEM] + [VMEM] * 5 + [HBM] * len(w),
        out_specs=(VMEM,) * 8,
        scratch_shapes=[pltpu.VMEM((4, 8, 64, 256), bf16), pltpu.VMEM(qf.shape, bf16), pltpu.SemaphoreType.DMA((32,))],
        cost_estimate=pl.CostEstimate(flops=2 * 512 * 256 * 2304, bytes_accessed=5 * 2**20, transcendentals=0),
        compiler_params=pltpu.CompilerParams(vmem_limit_bytes=LIMIT),
    )(ids, qf, num, den, before, gain, *w)


def gathered(own):
    mine = [shifted(own, "x", s) for s in SHIFTS]
    return mine + [swap(p) for p in mine]


def scattered(outs):
    sums = [m.astype(f32) + swap(o).astype(f32) for m, o in zip(outs[:4], outs[4:])]
    return sums[0] + sum(shifted(a.astype(bf16), "x", s).astype(f32) for a, s in zip(sums[1:], SHIFTS[1:]))


def local(hidden, qkv_weight, out_weight, projection, norm_gain, out_gain):
    layers = qkv_weight.shape[0]
    out_t = jnp.swapaxes(out_weight, 1, 2)
    weights, out_weights = weights_by_layer(qkv_weight, out_t)
    ids = group_ids()
    gain = norm_gain.reshape(layers * 8, 256)
    peers = lax.axis_size(SEQ)
    stream = hidden
    for l in range(layers):
        kf, v, state, scaled, inverse = project(l, ids, gathered(stream), gain, weights[l], projection)
        slices = lax.all_to_all(state.reshape(peers, 256 // peers, 256), SEQ, 0, 0, tiled=True).reshape(256, 256)
        qf = queries(l, ids, scaled, inverse, weights[l], projection)
        num, den = local_attention(qf, kf, v)
        sums = prefix(slices, peers).reshape(peers, 256 // peers, 256)
        before = lax.all_to_all(sums, SEQ, 0, 0, tiled=True).reshape(256, 256)
        outs = finish(l, ids, qf, num, den, before, out_gain, out_weights[l])
        stream = (stream.astype(f32) + scattered(outs)).astype(bf16)
    return stream


def solution(mesh):
    finer = Mesh(mesh.devices.reshape(4, 8, X, 2), ("y", "z", "x", "c"))
    in_specs = (
        P(SEQ, GRP),
        P(None, SEQ, GRP),
        P(None, GRP, SEQ),
        P(None, GRP, None, None),
        P(),
        P(None, GRP),
    )
    return jax.shard_map(local, mesh=finer, in_specs=in_specs, out_specs=P(SEQ, GRP), check_vma=False)
```

```python
import jax
import jax.numpy as jnp
from jax import lax
from jax.experimental import pallas as pl
from jax.experimental.pallas import tpu as pltpu
from jax.sharding import Mesh
from jax.sharding import PartitionSpec as P

SEQ = ("y", "z")
GRP = ("x", "c")
X = 4
ROWS = 256
TILE = 256
LIMIT = 48 * 2**20
STABILIZER = 2.0
bf16, f32 = jnp.bfloat16, jnp.float32
VMEM = pl.BlockSpec(memory_space=pltpu.VMEM)
SMEM = pl.BlockSpec(memory_space=pltpu.SMEM)
HBM = pl.BlockSpec(memory_space=pltpu.HBM)

SHIFTS = (0, 1, 3, 2)
SWAP = [(0, 1), (1, 0)]


def shifted(a, axis, by):
    n = lax.axis_size(axis)
    return lax.ppermute(a, axis, [(i, (i + by) % n) for i in range(n)]) if by else a


def swap(a):
    return lax.ppermute(a, "c", SWAP)


def group_ids():
    x, c = lax.axis_index("x"), lax.axis_index("c")
    came = [(x + X - s) % X * 2 + core for core in (c, 1 - c) for s in SHIFTS]
    goes = [(x + s) % X * 2 + core for core in (c, 1 - c) for s in SHIFTS]
    return jnp.stack(came + goes + [lax.axis_index("y"), lax.axis_index("z")]).astype(jnp.int32)


def dot(a, b, dims=((1,), (0,))):
    return lax.dot_general(a, b, (dims, ((), ())), preferred_element_type=f32)


def load_weights(ids, weights, w, first, sem):
    copies = []
    for i, dy in enumerate(SHIFTS):
        copy = pltpu.make_async_copy(
            weights.at[:, i, :, pl.ds(first, w.shape[-1])], w.at[(ids[16] + 4 - dy) % 4], sem.at[i]
        )
        copy.start()
        copies.append(copy)
    return copies


def weights_by_layer(shards):
    first = jnp.concatenate([shifted(shards[0], "y", s) for s in SHIFTS], axis=0)
    held, first = lax.optimization_barrier((jnp.concatenate(shards[1:], axis=0), first))
    later = [shifted(held, "y", s) for s in SHIFTS]
    columns = [first]
    for l in range(len(shards) - 1):
        columns.append(jnp.concatenate([p[64 * l : 64 * (l + 1)] for p in later], axis=0))
    return [lax.all_gather(c, "z", axis=0, tiled=True).reshape(8, 4, 64, 1024) for c in columns]


def project_kernel(layer, ids, *refs):
    parts, weights, refs = refs[:8], refs[8], refs[9:]
    gain, proj, qf_ref, kf_ref, v_ref, state_ref, w, scaled, squares, state, pair, low, sem = refs
    copies = load_weights(ids, weights, w, 0, sem)
    for n in range(2):
        part = proj[layer, n] * 128 ** (-0.25)
        high = part.astype(bf16)
        rest = part - high.astype(f32)
        mid = rest.astype(bf16)
        pair[n, :, :128] = high
        pair[n, :, 128:] = mid
        low[n] = (rest - mid.astype(f32)).astype(bf16)
    tokens = parts[0].shape[0]
    gains = [gain[pl.ds(layer * 8 + ids[k], 1), :] for k in range(8)]
    state[...] = jnp.zeros_like(state)

    @pl.loop(0, tokens // 64)
    def _(i):
        rows = pl.ds(pl.multiple_of(i * 64, 64), 64)
        total = jnp.zeros((64, 256), f32)
        for k in range(8):
            wide = parts[k][rows, :].astype(f32)
            total += wide * wide
            scaled[rows, pl.ds(pl.multiple_of(ids[k] * 256, 256), 256)] = (wide * gains[k]).astype(bf16)
        squares[rows, :] = total[:, :128] + total[:, 128:]

    for copy in copies:
        copy.wait()
    ones = jnp.ones((TILE, 128), bf16)

    @pl.loop(0, tokens // TILE)
    def _(i):
        rows = pl.ds(pl.multiple_of(i * TILE, TILE), TILE)
        inverse_rms = lax.rsqrt(jnp.sum(squares[rows, :], axis=-1, keepdims=True) * (1.0 / 2048) + 1e-05)
        qkv = (dot(scaled[rows, :], w[...].reshape(2048, 768)) * inverse_rms).astype(bf16)
        for n in range(2):
            feats = []
            for j in range(2):
                u = qkv[:, n * 384 + j * 128 : n * 384 + (j + 1) * 128]
                both = dot(u, pair[n])
                mixed = both[:, :128] + (both[:, 128:] + dot(u, low[n]))
                uw = u.astype(f32)
                energy = jnp.sum(uw * uw, axis=-1, keepdims=True) * (0.5 * 128 ** (-0.5))
                feats.append((jnp.exp(mixed - energy - STABILIZER) * 128 ** (-0.5)).astype(bf16))
            value = qkv[:, n * 384 + 256 : n * 384 + 384]
            cols = pl.ds(n * 128, 128)
            qf_ref[rows, cols] = feats[0]
            kf_ref[rows, cols] = feats[1]
            v_ref[rows, cols] = value
            state[cols, :] += dot(feats[1], jnp.concatenate([value, ones], axis=1), ((0,), (0,)))

    state_ref[...] = state[...].astype(bf16)


def project(layer, ids, parts, gain, w, proj):
    tokens = parts[0].shape[0]
    half = jax.ShapeDtypeStruct((tokens, 256), bf16)
    return pl.pallas_call(
        lambda *refs: project_kernel(layer, *refs),
        name="project",
        out_shape=(half, half, half, jax.ShapeDtypeStruct((256, 256), bf16)),
        in_specs=[SMEM] + [VMEM] * 8 + [HBM] + [VMEM] * 2,
        out_specs=(VMEM,) * 4,
        scratch_shapes=[
            pltpu.VMEM((4, 8, 64, 768), bf16),
            pltpu.VMEM((tokens, 2048), bf16),
            pltpu.VMEM((tokens, 128), f32),
            pltpu.VMEM((256, 256), f32),
            pltpu.VMEM((2, 128, 256), bf16),
            pltpu.VMEM((2, 128, 128), bf16),
            pltpu.SemaphoreType.DMA((4,)),
        ],
        cost_estimate=pl.CostEstimate(flops=2 * 512 * 2048 * 768, bytes_accessed=6 * 2**20, transcendentals=0),
        compiler_params=pltpu.CompilerParams(vmem_limit_bytes=LIMIT),
    )(ids, *parts, w, gain, proj)


def local_kernel(qf, kf, v, num_ref, den_ref):
    tile = 256
    keep = lax.broadcasted_iota(jnp.int32, (tile, tile), 0) >= lax.broadcasted_iota(jnp.int32, (tile, tile), 1)
    for n in range(2):
        cols = pl.ds(n * 128, 128)
        for i in range(qf.shape[0] // tile):
            rows = pl.ds(i * tile, tile)
            num = jnp.zeros((tile, 128), f32)
            den = jnp.zeros((tile, 1), f32)
            for j in range(i + 1):
                keys = pl.ds(j * tile, tile)
                scores = dot(qf[rows, cols], kf[keys, cols], ((1,), (1,)))
                if j == i:
                    scores = jnp.where(keep, scores, 0.0)
                den += jnp.sum(scores, axis=-1, keepdims=True)
                num += dot(scores.astype(bf16), v[keys, cols])
            num_ref[rows, cols] = num
            den_ref[rows, cols] = jnp.broadcast_to(den, (tile, 128))


def local_attention(qf, kf, v):
    whole = jax.ShapeDtypeStruct(qf.shape, f32)
    return pl.pallas_call(
        local_kernel,
        name="local_attention",
        out_shape=(whole, whole),
        in_specs=[VMEM] * 3,
        out_specs=(VMEM,) * 2,
        cost_estimate=pl.CostEstimate(flops=2 * 4 * 512 * 512 * 128, bytes_accessed=2 * 2**20, transcendentals=0),
        compiler_params=pltpu.CompilerParams(vmem_limit_bytes=LIMIT),
    )(qf, kf, v)


def prefix_kernel(peers, in_ref, out_ref):
    n = in_ref.shape[0]
    width = n // peers
    row = lax.broadcasted_iota(jnp.int32, (n, n), 0)
    col = lax.broadcasted_iota(jnp.int32, (n, n), 1)
    earlier = (col < (row & -width)) & (((row ^ col) & (width - 1)) == 0)
    out_ref[...] = dot(earlier.astype(f32).astype(bf16), in_ref[...]).astype(bf16)


def prefix(slices, peers):
    return pl.pallas_call(
        lambda *refs: prefix_kernel(peers, *refs),
        name="prefix",
        out_shape=jax.ShapeDtypeStruct(slices.shape, bf16),
        in_specs=[VMEM],
        out_specs=VMEM,
        compiler_params=pltpu.CompilerParams(vmem_limit_bytes=LIMIT),
    )(slices)


def finish_kernel(layer, ids, qf, num, den, before, gain, *refs):
    weights, outs = refs[0], refs[1:9]
    w, sem = refs[-2:]
    copies = load_weights(ids, weights, w, 768, sem)

    for copy in copies:
        copy.wait()

    @pl.loop(0, qf.shape[0] // ROWS)
    def _(i):
        rows = pl.ds(pl.multiple_of(i * ROWS, ROWS), ROWS)
        heads = []
        for n in range(2):
            cols = pl.ds(n * 128, 128)
            both = dot(qf[rows, cols], before[cols, :])
            attention = (num[rows, cols] + both[:, :128]) / (den[rows, cols] + both[:, 128:])
            inverse = lax.rsqrt(jnp.sum(attention * attention, axis=-1, keepdims=True) * (1.0 / 128) + 1e-06)
            heads.append((attention * inverse * gain[pl.ds(layer, 1), cols]).astype(bf16))
        attended = jnp.concatenate(heads, axis=1)
        for k in range(8):
            group = ids[8 + k]
            part = w[group // 2, pl.ds(group % 2 * 4, 4)].reshape(256, 256)
            outs[k][rows, :] = dot(attended, part, ((1,), (1,))).astype(bf16)


def finish(layer, ids, qf, num, den, before, gain, w):
    part = jax.ShapeDtypeStruct(qf.shape, bf16)
    return pl.pallas_call(
        lambda *refs: finish_kernel(layer, *refs),
        name="finish",
        out_shape=(part,) * 8,
        in_specs=[SMEM] + [VMEM] * 5 + [HBM],
        out_specs=(VMEM,) * 8,
        scratch_shapes=[pltpu.VMEM((4, 8, 64, 256), bf16), pltpu.SemaphoreType.DMA((4,))],
        cost_estimate=pl.CostEstimate(flops=2 * 512 * 256 * 2304, bytes_accessed=5 * 2**20, transcendentals=0),
        compiler_params=pltpu.CompilerParams(vmem_limit_bytes=LIMIT),
    )(ids, qf, num, den, before, gain, w)


def gathered(own):
    mine = [shifted(own, "x", s) for s in SHIFTS]
    return mine + [swap(p) for p in mine]


def scattered(outs):
    sums = [m.astype(f32) + swap(o).astype(f32) for m, o in zip(outs[:4], outs[4:])]
    return sums[0] + sum(shifted(a.astype(bf16), "x", s).astype(f32) for a, s in zip(sums[1:], SHIFTS[1:]))


def local(hidden, qkv_weight, out_weight, projection, norm_gain, out_gain):
    layers = qkv_weight.shape[0]
    out_t = jnp.swapaxes(out_weight, 1, 2)
    shards = [jnp.concatenate([qkv_weight[l], out_t[l]], axis=1) for l in range(layers)]
    weights = weights_by_layer(shards)
    ids = group_ids()
    gain = norm_gain.reshape(layers * 8, 256)
    peers = lax.axis_size(SEQ)
    stream = hidden
    for l in range(layers):
        qf, kf, v, state = project(l, ids, gathered(stream), gain, weights[l], projection)
        slices = lax.all_to_all(state.reshape(peers, 256 // peers, 256), SEQ, 0, 0, tiled=True).reshape(256, 256)
        num, den = local_attention(qf, kf, v)
        sums = prefix(slices, peers).reshape(peers, 256 // peers, 256)
        before = lax.all_to_all(sums, SEQ, 0, 0, tiled=True).reshape(256, 256)
        outs = finish(l, ids, qf, num, den, before, out_gain, weights[l])
        stream = (stream.astype(f32) + scattered(outs)).astype(bf16)
    return stream


def solution(mesh):
    finer = Mesh(mesh.devices.reshape(4, 8, X, 2), ("y", "z", "x", "c"))
    in_specs = (
        P(SEQ, GRP),
        P(None, SEQ, GRP),
        P(None, GRP, SEQ),
        P(None, GRP, None, None),
        P(),
        P(None, GRP),
    )
    return jax.shard_map(local, mesh=finer, in_specs=in_specs, out_specs=P(SEQ, GRP), check_vma=False)
```

```python
import jax
import jax.numpy as jnp
from jax import lax
from jax.experimental import pallas as pl
from jax.experimental.pallas import tpu as pltpu
from jax.sharding import Mesh
from jax.sharding import PartitionSpec as P

SEQ = ("y", "z")
GRP = ("x", "c")
X = 4
TILE = 512
LIMIT = 48 * 2**20
STABILIZER = 2.0
bf16, f32 = jnp.bfloat16, jnp.float32
VMEM = pl.BlockSpec(memory_space=pltpu.VMEM)
SMEM = pl.BlockSpec(memory_space=pltpu.SMEM)
HBM = pl.BlockSpec(memory_space=pltpu.HBM)

SHIFTS = (0, 1, 3, 2)
SWAP = [(0, 1), (1, 0)]


def shifted(a, axis, by):
    n = lax.axis_size(axis)
    return lax.ppermute(a, axis, [(i, (i + by) % n) for i in range(n)]) if by else a


def swap(a):
    return lax.ppermute(a, "c", SWAP)


def group_ids():
    x, c = lax.axis_index("x"), lax.axis_index("c")
    came = [(x + X - s) % X * 2 + core for core in (c, 1 - c) for s in SHIFTS]
    goes = [(x + s) % X * 2 + core for core in (c, 1 - c) for s in SHIFTS]
    return jnp.stack(came + goes + [lax.axis_index("y"), lax.axis_index("z")]).astype(jnp.int32)


def dot(a, b, dims=((1,), (0,))):
    return lax.dot_general(a, b, (dims, ((), ())), preferred_element_type=f32)


def load_weights(ids, weights, w, first, sem):
    copies = []
    for i, dy in enumerate(SHIFTS):
        copy = pltpu.make_async_copy(
            weights.at[:, i, :, pl.ds(first, w.shape[-1])], w.at[(ids[16] + 4 - dy) % 4], sem.at[i]
        )
        copy.start()
        copies.append(copy)
    return copies


def weights_by_layer(shards):
    first = jnp.concatenate([shifted(shards[0], "y", s) for s in SHIFTS], axis=0)
    held, first = lax.optimization_barrier((jnp.concatenate(shards[1:], axis=0), first))
    later = [shifted(held, "y", s) for s in SHIFTS]
    columns = [first]
    for l in range(len(shards) - 1):
        columns.append(jnp.concatenate([p[64 * l : 64 * (l + 1)] for p in later], axis=0))
    return [lax.all_gather(c, "z", axis=0, tiled=True).reshape(8, 4, 64, 1024) for c in columns]


def project_kernel(layer, ids, *refs):
    parts, weights, refs = refs[:8], refs[8], refs[9:]
    gain, proj, qf_ref, kf_ref, v_ref, state_ref, w, scaled, squares, state, pair, low, sem = refs
    copies = load_weights(ids, weights, w, 0, sem)
    for n in range(2):
        part = proj[layer, n] * 128 ** (-0.25)
        high = part.astype(bf16)
        rest = part - high.astype(f32)
        mid = rest.astype(bf16)
        pair[n, :, :128] = high
        pair[n, :, 128:] = mid
        low[n] = (rest - mid.astype(f32)).astype(bf16)
    tokens = parts[0].shape[0]
    gains = [gain[pl.ds(layer * 8 + ids[k], 1), :] for k in range(8)]
    state[...] = jnp.zeros_like(state)

    @pl.loop(0, tokens // 64)
    def _(i):
        rows = pl.ds(pl.multiple_of(i * 64, 64), 64)
        total = jnp.zeros((64, 256), f32)
        for k in range(8):
            wide = parts[k][rows, :].astype(f32)
            total += wide * wide
            scaled[rows, pl.ds(pl.multiple_of(ids[k] * 256, 256), 256)] = (wide * gains[k]).astype(bf16)
        squares[rows, :] = total[:, :128] + total[:, 128:]

    for copy in copies:
        copy.wait()
    ones = jnp.ones((TILE, 128), bf16)

    @pl.loop(0, tokens // TILE)
    def _(i):
        rows = pl.ds(pl.multiple_of(i * TILE, TILE), TILE)
        inverse_rms = lax.rsqrt(jnp.sum(squares[rows, :], axis=-1, keepdims=True) * (1.0 / 2048) + 1e-05)
        qkv = (dot(scaled[rows, :], w[...].reshape(2048, 768)) * inverse_rms).astype(bf16)
        for n in range(2):
            feats = []
            for j in range(2):
                u = qkv[:, n * 384 + j * 128 : n * 384 + (j + 1) * 128]
                both = dot(u, pair[n])
                mixed = both[:, :128] + (both[:, 128:] + dot(u, low[n]))
                uw = u.astype(f32)
                energy = jnp.sum(uw * uw, axis=-1, keepdims=True) * (0.5 * 128 ** (-0.5))
                feats.append((jnp.exp(mixed - energy - STABILIZER) * 128 ** (-0.5)).astype(bf16))
            value = qkv[:, n * 384 + 256 : n * 384 + 384]
            cols = pl.ds(n * 128, 128)
            qf_ref[rows, cols] = feats[0]
            kf_ref[rows, cols] = feats[1]
            v_ref[rows, cols] = value
            state[cols, :] += dot(feats[1], jnp.concatenate([value, ones], axis=1), ((0,), (0,)))

    state_ref[...] = state[...].astype(bf16)


def project(layer, ids, parts, gain, w, proj):
    tokens = parts[0].shape[0]
    half = jax.ShapeDtypeStruct((tokens, 256), bf16)
    return pl.pallas_call(
        lambda *refs: project_kernel(layer, *refs),
        name="project",
        out_shape=(half, half, half, jax.ShapeDtypeStruct((256, 256), bf16)),
        in_specs=[SMEM] + [VMEM] * 8 + [HBM] + [VMEM] * 2,
        out_specs=(VMEM,) * 4,
        scratch_shapes=[
            pltpu.VMEM((4, 8, 64, 768), bf16),
            pltpu.VMEM((tokens, 2048), bf16),
            pltpu.VMEM((tokens, 128), f32),
            pltpu.VMEM((256, 256), f32),
            pltpu.VMEM((2, 128, 256), bf16),
            pltpu.VMEM((2, 128, 128), bf16),
            pltpu.SemaphoreType.DMA((4,)),
        ],
        cost_estimate=pl.CostEstimate(flops=2 * 512 * 2048 * 768, bytes_accessed=6 * 2**20, transcendentals=0),
        compiler_params=pltpu.CompilerParams(vmem_limit_bytes=LIMIT),
    )(ids, *parts, w, gain, proj)


def local_kernel(qf, kf, v, num_ref, den_ref):
    tile = 256
    keep = lax.broadcasted_iota(jnp.int32, (tile, tile), 0) >= lax.broadcasted_iota(jnp.int32, (tile, tile), 1)
    for n in range(2):
        cols = pl.ds(n * 128, 128)
        for i in range(qf.shape[0] // tile):
            rows = pl.ds(i * tile, tile)
            num = jnp.zeros((tile, 128), f32)
            den = jnp.zeros((tile, 1), f32)
            for j in range(i + 1):
                keys = pl.ds(j * tile, tile)
                scores = dot(qf[rows, cols], kf[keys, cols], ((1,), (1,)))
                if j == i:
                    scores = jnp.where(keep, scores, 0.0)
                den += jnp.sum(scores, axis=-1, keepdims=True)
                num += dot(scores.astype(bf16), v[keys, cols])
            num_ref[rows, cols] = num
            den_ref[rows, cols] = jnp.broadcast_to(den, (tile, 128))


def local_attention(qf, kf, v):
    whole = jax.ShapeDtypeStruct(qf.shape, f32)
    return pl.pallas_call(
        local_kernel,
        name="local_attention",
        out_shape=(whole, whole),
        in_specs=[VMEM] * 3,
        out_specs=(VMEM,) * 2,
        cost_estimate=pl.CostEstimate(flops=2 * 4 * 512 * 512 * 128, bytes_accessed=2 * 2**20, transcendentals=0),
        compiler_params=pltpu.CompilerParams(vmem_limit_bytes=LIMIT),
    )(qf, kf, v)


def prefix_kernel(peers, in_ref, out_ref):
    n = in_ref.shape[0]
    width = n // peers
    row = lax.broadcasted_iota(jnp.int32, (n, n), 0)
    col = lax.broadcasted_iota(jnp.int32, (n, n), 1)
    earlier = (col < (row & -width)) & (((row ^ col) & (width - 1)) == 0)
    out_ref[...] = dot(earlier.astype(f32).astype(bf16), in_ref[...]).astype(bf16)


def prefix(slices, peers):
    return pl.pallas_call(
        lambda *refs: prefix_kernel(peers, *refs),
        name="prefix",
        out_shape=jax.ShapeDtypeStruct(slices.shape, bf16),
        in_specs=[VMEM],
        out_specs=VMEM,
        compiler_params=pltpu.CompilerParams(vmem_limit_bytes=LIMIT),
    )(slices)


def finish_kernel(layer, ids, qf, num, den, before, gain, *refs):
    weights, outs = refs[0], refs[1:9]
    w, attended, sem = refs[-3:]
    copies = load_weights(ids, weights, w, 768, sem)

    for n in range(2):
        cols = pl.ds(n * 128, 128)
        both = dot(qf[:, cols], before[cols, :])
        attention = (num[:, cols] + both[:, :128]) / (den[:, cols] + both[:, 128:])
        inverse = lax.rsqrt(jnp.sum(attention * attention, axis=-1, keepdims=True) * (1.0 / 128) + 1e-06)
        attended[:, cols] = (attention * inverse * gain[pl.ds(layer, 1), cols]).astype(bf16)
    for copy in copies:
        copy.wait()
    for k in range(8):
        group = ids[8 + k]
        part = w[group // 2, pl.ds(group % 2 * 4, 4)].reshape(256, 256)
        outs[k][...] = dot(attended[...], part, ((1,), (1,))).astype(bf16)


def finish(layer, ids, qf, num, den, before, gain, w):
    part = jax.ShapeDtypeStruct(qf.shape, bf16)
    return pl.pallas_call(
        lambda *refs: finish_kernel(layer, *refs),
        name="finish",
        out_shape=(part,) * 8,
        in_specs=[SMEM] + [VMEM] * 5 + [HBM],
        out_specs=(VMEM,) * 8,
        scratch_shapes=[pltpu.VMEM((4, 8, 64, 256), bf16), pltpu.VMEM(qf.shape, bf16), pltpu.SemaphoreType.DMA((4,))],
        cost_estimate=pl.CostEstimate(flops=2 * 512 * 256 * 2304, bytes_accessed=5 * 2**20, transcendentals=0),
        compiler_params=pltpu.CompilerParams(vmem_limit_bytes=LIMIT),
    )(ids, qf, num, den, before, gain, w)


def gathered(own):
    mine = [shifted(own, "x", s) for s in SHIFTS]
    return mine + [swap(p) for p in mine]


def scattered(outs):
    sums = [m.astype(f32) + swap(o).astype(f32) for m, o in zip(outs[:4], outs[4:])]
    return sums[0] + sum(shifted(a.astype(bf16), "x", s).astype(f32) for a, s in zip(sums[1:], SHIFTS[1:]))


def local(hidden, qkv_weight, out_weight, projection, norm_gain, out_gain):
    layers = qkv_weight.shape[0]
    out_t = jnp.swapaxes(out_weight, 1, 2)
    shards = [jnp.concatenate([qkv_weight[l], out_t[l]], axis=1) for l in range(layers)]
    weights = weights_by_layer(shards)
    ids = group_ids()
    gain = norm_gain.reshape(layers * 8, 256)
    peers = lax.axis_size(SEQ)
    stream = hidden
    for l in range(layers):
        qf, kf, v, state = project(l, ids, gathered(stream), gain, weights[l], projection)
        slices = lax.all_to_all(state.reshape(peers, 256 // peers, 256), SEQ, 0, 0, tiled=True).reshape(256, 256)
        num, den = local_attention(qf, kf, v)
        sums = prefix(slices, peers).reshape(peers, 256 // peers, 256)
        before = lax.all_to_all(sums, SEQ, 0, 0, tiled=True).reshape(256, 256)
        outs = finish(l, ids, qf, num, den, before, out_gain, weights[l])
        stream = (stream.astype(f32) + scattered(outs)).astype(bf16)
    return stream


def solution(mesh):
    finer = Mesh(mesh.devices.reshape(4, 8, X, 2), ("y", "z", "x", "c"))
    in_specs = (
        P(SEQ, GRP),
        P(None, SEQ, GRP),
        P(None, GRP, SEQ),
        P(None, GRP, None, None),
        P(),
        P(None, GRP),
    )
    return jax.shard_map(local, mesh=finer, in_specs=in_specs, out_specs=P(SEQ, GRP), check_vma=False)
```

```python
import jax
import jax.numpy as jnp
from jax import lax
from jax.experimental import pallas as pl
from jax.experimental.pallas import tpu as pltpu
from jax.sharding import Mesh
from jax.sharding import PartitionSpec as P

SEQ = ("y", "z")
GRP = ("x", "c")
X = 4
TILE = 512
LIMIT = 48 * 2**20
STABILIZER = 2.0
bf16, f32 = jnp.bfloat16, jnp.float32
VMEM = pl.BlockSpec(memory_space=pltpu.VMEM)
SMEM = pl.BlockSpec(memory_space=pltpu.SMEM)
ANY = pl.BlockSpec(memory_space=pl.ANY)
HBM = pl.BlockSpec(memory_space=pltpu.HBM)

SHIFTS = (0, 1, 3, 2)
SWAP = [(0, 1), (1, 0)]


def shifted(a, axis, by):
    n = lax.axis_size(axis)
    return lax.ppermute(a, axis, [(i, (i + by) % n) for i in range(n)]) if by else a


def swap(a):
    return lax.ppermute(a, "c", SWAP)


def group_ids():
    x, c = lax.axis_index("x"), lax.axis_index("c")
    came = [(x + X - s) % X * 2 + core for core in (c, 1 - c) for s in SHIFTS]
    goes = [(x + s) % X * 2 + core for core in (c, 1 - c) for s in SHIFTS]
    return jnp.stack(came + goes + [lax.axis_index("y"), lax.axis_index("z")]).astype(jnp.int32)


def dot(a, b, dims=((1,), (0,))):
    return lax.dot_general(a, b, (dims, ((), ())), preferred_element_type=f32)


def load_weights(ids, weights, w, first, sem):
    copies = []
    for i, dy in enumerate(SHIFTS):
        copy = pltpu.make_async_copy(
            weights.at[:, i, :, pl.ds(first, w.shape[-1])], w.at[(ids[16] + 4 - dy) % 4], sem.at[i]
        )
        copy.start()
        copies.append(copy)
    return copies


def gathered_over_z(column):
    whole = lax.all_gather(column.reshape(256, -1), "z", axis=0, tiled=True)
    return whole.reshape(8, 4, 64, -1)


def columns_of_weights(qkv_weight, out_t):
    first = jnp.concatenate([qkv_weight[0], out_t[0]], axis=1)
    first = jnp.stack([shifted(first, "y", s) for s in SHIFTS])
    qkv_weight, out_t, first = lax.optimization_barrier((qkv_weight, out_t, first))
    held = jnp.concatenate([jnp.concatenate([qkv_weight[l], out_t[l]], axis=1) for l in (1, 2)], axis=0)
    later = [shifted(held, "y", s) for s in SHIFTS]
    columns = [jnp.stack([p[64 * l : 64 * (l + 1)] for p in later]) for l in range(2)]
    return first[:, :, :768], first[:, :, 768:], columns


RELAYED = ((0, 0, 0), (1, 0, 1), (2, 0, 7), (3, 0, 2), (4, 0, 6), (5, 0, 3), (6, 0, 5), (7, 0, 4), (8, 2, 4))


def relayed(column):
    up = down = column
    out = [column]
    for _ in range(3):
        up, down = shifted(up, "z", 1), shifted(down, "z", 7)
        out += [up, down]
    return out + [shifted(up[:2], "z", 1), shifted(down[2:], "z", 7)]


def load_relayed(ids, weights, w, sem):
    copies = []
    for ref, low, dz in RELAYED:
        for i in range(low, low + weights[ref].shape[0]):
            at = (ids[16] + 4 - SHIFTS[i]) % 4
            copy = pltpu.make_async_copy(
                weights[ref].at[i - low], w.at[at, (ids[17] + 8 - dz) % 8], sem.at[len(copies)]
            )
            copy.start()
            copies.append(copy)
    return copies


def project_kernel(layer, ids, *refs):
    parts, weights, refs = refs[:8], refs[8], refs[9:]
    gain, proj, qf_ref, kf_ref, v_ref, state_ref, w, scaled, squares, state, pair, low, sem = refs
    copies = load_weights(ids, weights, w, 0, sem)
    for n in range(2):
        part = proj[layer, n] * 128 ** (-0.25)
        high = part.astype(bf16)
        rest = part - high.astype(f32)
        mid = rest.astype(bf16)
        pair[n, :, :128] = high
        pair[n, :, 128:] = mid
        low[n] = (rest - mid.astype(f32)).astype(bf16)
    tokens = parts[0].shape[0]
    gains = [gain[pl.ds(layer * 8 + ids[k], 1), :] for k in range(8)]
    state[...] = jnp.zeros_like(state)

    @pl.loop(0, tokens // 64)
    def _(i):
        rows = pl.ds(pl.multiple_of(i * 64, 64), 64)
        total = jnp.zeros((64, 256), f32)
        for k in range(8):
            wide = parts[k][rows, :].astype(f32)
            total += wide * wide
            scaled[rows, pl.ds(pl.multiple_of(ids[k] * 256, 256), 256)] = (wide * gains[k]).astype(bf16)
        squares[rows, :] = total[:, :128] + total[:, 128:]

    for copy in copies:
        copy.wait()
    ones = jnp.ones((TILE, 128), bf16)

    @pl.loop(0, tokens // TILE)
    def _(i):
        rows = pl.ds(pl.multiple_of(i * TILE, TILE), TILE)
        inverse_rms = lax.rsqrt(jnp.sum(squares[rows, :], axis=-1, keepdims=True) * (1.0 / 2048) + 1e-05)
        qkv = (dot(scaled[rows, :], w[...].reshape(2048, 768)) * inverse_rms).astype(bf16)
        for n in range(2):
            feats = []
            for j in range(2):
                u = qkv[:, n * 384 + j * 128 : n * 384 + (j + 1) * 128]
                both = dot(u, pair[n])
                mixed = both[:, :128] + (both[:, 128:] + dot(u, low[n]))
                uw = u.astype(f32)
                energy = jnp.sum(uw * uw, axis=-1, keepdims=True) * (0.5 * 128 ** (-0.5))
                feats.append((jnp.exp(mixed - energy - STABILIZER) * 128 ** (-0.5)).astype(bf16))
            value = qkv[:, n * 384 + 256 : n * 384 + 384]
            cols = pl.ds(n * 128, 128)
            qf_ref[rows, cols] = feats[0]
            kf_ref[rows, cols] = feats[1]
            v_ref[rows, cols] = value
            state[cols, :] += dot(feats[1], jnp.concatenate([value, ones], axis=1), ((0,), (0,)))

    state_ref[...] = state[...].astype(bf16)


def project(layer, ids, parts, gain, w, proj):
    tokens = parts[0].shape[0]
    half = jax.ShapeDtypeStruct((tokens, 256), bf16)
    return pl.pallas_call(
        lambda *refs: project_kernel(layer, *refs),
        name="project",
        out_shape=(half, half, half, jax.ShapeDtypeStruct((256, 256), bf16)),
        in_specs=[SMEM] + [VMEM] * 8 + [HBM] + [VMEM] * 2,
        out_specs=(VMEM,) * 4,
        scratch_shapes=[
            pltpu.VMEM((4, 8, 64, 768), bf16),
            pltpu.VMEM((tokens, 2048), bf16),
            pltpu.VMEM((tokens, 128), f32),
            pltpu.VMEM((256, 256), f32),
            pltpu.VMEM((2, 128, 256), bf16),
            pltpu.VMEM((2, 128, 128), bf16),
            pltpu.SemaphoreType.DMA((4,)),
        ],
        cost_estimate=pl.CostEstimate(flops=2 * 512 * 2048 * 768, bytes_accessed=6 * 2**20, transcendentals=0),
        compiler_params=pltpu.CompilerParams(vmem_limit_bytes=LIMIT),
    )(ids, *parts, w, gain, proj)


def local_kernel(qf, kf, v, num_ref, den_ref):
    tile = 256
    keep = lax.broadcasted_iota(jnp.int32, (tile, tile), 0) >= lax.broadcasted_iota(jnp.int32, (tile, tile), 1)
    for n in range(2):
        cols = pl.ds(n * 128, 128)
        for i in range(qf.shape[0] // tile):
            rows = pl.ds(i * tile, tile)
            num = jnp.zeros((tile, 128), f32)
            den = jnp.zeros((tile, 1), f32)
            for j in range(i + 1):
                keys = pl.ds(j * tile, tile)
                scores = dot(qf[rows, cols], kf[keys, cols], ((1,), (1,)))
                if j == i:
                    scores = jnp.where(keep, scores, 0.0)
                den += jnp.sum(scores, axis=-1, keepdims=True)
                num += dot(scores.astype(bf16), v[keys, cols])
            num_ref[rows, cols] = num
            den_ref[rows, cols] = jnp.broadcast_to(den, (tile, 128))


def local_attention(qf, kf, v):
    whole = jax.ShapeDtypeStruct(qf.shape, f32)
    return pl.pallas_call(
        local_kernel,
        name="local_attention",
        out_shape=(whole, whole),
        in_specs=[VMEM] * 3,
        out_specs=(VMEM,) * 2,
        cost_estimate=pl.CostEstimate(flops=2 * 4 * 512 * 512 * 128, bytes_accessed=2 * 2**20, transcendentals=0),
        compiler_params=pltpu.CompilerParams(vmem_limit_bytes=LIMIT),
    )(qf, kf, v)


def prefix_kernel(peers, in_ref, out_ref):
    n = in_ref.shape[0]
    width = n // peers
    row = lax.broadcasted_iota(jnp.int32, (n, n), 0)
    col = lax.broadcasted_iota(jnp.int32, (n, n), 1)
    earlier = (col < (row & -width)) & (((row ^ col) & (width - 1)) == 0)
    out_ref[...] = dot(earlier.astype(f32).astype(bf16), in_ref[...]).astype(bf16)


def prefix(slices, peers):
    return pl.pallas_call(
        lambda *refs: prefix_kernel(peers, *refs),
        name="prefix",
        out_shape=jax.ShapeDtypeStruct(slices.shape, bf16),
        in_specs=[VMEM],
        out_specs=VMEM,
        compiler_params=pltpu.CompilerParams(vmem_limit_bytes=LIMIT),
    )(slices)


def finish_kernel(layer, ids, qf, num, den, before, gain, *refs):
    weights, outs = refs[:-11], refs[-11:-3]
    w, attended, sem = refs[-3:]
    if len(weights) == 1:
        copies = load_weights(ids, weights[0], w, 768, sem)
    else:
        copies = load_relayed(ids, weights, w, sem)

    for n in range(2):
        cols = pl.ds(n * 128, 128)
        both = dot(qf[:, cols], before[cols, :])
        attention = (num[:, cols] + both[:, :128]) / (den[:, cols] + both[:, 128:])
        inverse = lax.rsqrt(jnp.sum(attention * attention, axis=-1, keepdims=True) * (1.0 / 128) + 1e-06)
        attended[:, cols] = (attention * inverse * gain[pl.ds(layer, 1), cols]).astype(bf16)
    for copy in copies:
        copy.wait()
    for k in range(8):
        group = ids[8 + k]
        part = w[group // 2, pl.ds(group % 2 * 4, 4)].reshape(256, 256)
        outs[k][...] = dot(attended[...], part, ((1,), (1,))).astype(bf16)


def finish(layer, ids, qf, num, den, before, gain, w):
    part = jax.ShapeDtypeStruct(qf.shape, bf16)
    return pl.pallas_call(
        lambda *refs: finish_kernel(layer, *refs),
        name="finish",
        out_shape=(part,) * 8,
        in_specs=[SMEM] + [VMEM] * 5 + [HBM if len(w) == 1 else ANY] * len(w),
        out_specs=(VMEM,) * 8,
        scratch_shapes=[pltpu.VMEM((4, 8, 64, 256), bf16), pltpu.VMEM(qf.shape, bf16), pltpu.SemaphoreType.DMA((32,))],
        cost_estimate=pl.CostEstimate(flops=2 * 512 * 256 * 2304, bytes_accessed=5 * 2**20, transcendentals=0),
        compiler_params=pltpu.CompilerParams(vmem_limit_bytes=LIMIT),
    )(ids, qf, num, den, before, gain, *w)


def gathered(own):
    mine = [shifted(own, "x", s) for s in SHIFTS]
    return mine + [swap(p) for p in mine]


def scattered(outs):
    sums = [m.astype(f32) + swap(o).astype(f32) for m, o in zip(outs[:4], outs[4:])]
    return sums[0] + sum(shifted(a.astype(bf16), "x", s).astype(f32) for a, s in zip(sums[1:], SHIFTS[1:]))


def local(hidden, qkv_weight, out_weight, projection, norm_gain, out_gain):
    layers = qkv_weight.shape[0]
    out_t = jnp.swapaxes(out_weight, 1, 2)
    first, out_first, columns = columns_of_weights(qkv_weight, out_t)
    weights = [gathered_over_z(c) for c in (first, *columns)]
    out_weights = [None] + [[w] for w in weights[1:]]
    ids = group_ids()
    gain = norm_gain.reshape(layers * 8, 256)
    peers = lax.axis_size(SEQ)
    stream = hidden
    for l in range(layers):
        qf, kf, v, state = project(l, ids, gathered(stream), gain, weights[l], projection)
        if l == 0:
            out_first, state = lax.optimization_barrier((out_first, state))
            out_weights[0] = relayed(out_first)
        slices = lax.all_to_all(state.reshape(peers, 256 // peers, 256), SEQ, 0, 0, tiled=True).reshape(256, 256)
        num, den = local_attention(qf, kf, v)
        sums = prefix(slices, peers).reshape(peers, 256 // peers, 256)
        before = lax.all_to_all(sums, SEQ, 0, 0, tiled=True).reshape(256, 256)
        outs = finish(l, ids, qf, num, den, before, out_gain, out_weights[l])
        stream = (stream.astype(f32) + scattered(outs)).astype(bf16)
    return stream


def solution(mesh):
    finer = Mesh(mesh.devices.reshape(4, 8, X, 2), ("y", "z", "x", "c"))
    in_specs = (
        P(SEQ, GRP),
        P(None, SEQ, GRP),
        P(None, GRP, SEQ),
        P(None, GRP, None, None),
        P(),
        P(None, GRP),
    )
    return jax.shard_map(local, mesh=finer, in_specs=in_specs, out_specs=P(SEQ, GRP), check_vma=False)
```

```python
import jax
import jax.numpy as jnp
from jax import lax
from jax.experimental import pallas as pl
from jax.experimental.pallas import tpu as pltpu
from jax.sharding import Mesh
from jax.sharding import PartitionSpec as P

SEQ = ("y", "z")
GRP = ("x", "c")
X = 4
TILE = 512
LIMIT = 48 * 2**20
STABILIZER = 2.0
bf16, f32 = jnp.bfloat16, jnp.float32
VMEM = pl.BlockSpec(memory_space=pltpu.VMEM)
SMEM = pl.BlockSpec(memory_space=pltpu.SMEM)
HBM = pl.BlockSpec(memory_space=pltpu.HBM)

SHIFTS = (0, 1, 3, 2)
SWAP = [(0, 1), (1, 0)]


def shifted(a, axis, by):
    n = lax.axis_size(axis)
    return lax.ppermute(a, axis, [(i, (i + by) % n) for i in range(n)]) if by else a


def swap(a):
    return lax.ppermute(a, "c", SWAP)


def group_ids():
    x, c = lax.axis_index("x"), lax.axis_index("c")
    came = [(x + X - s) % X * 2 + core for core in (c, 1 - c) for s in SHIFTS]
    goes = [(x + s) % X * 2 + core for core in (c, 1 - c) for s in SHIFTS]
    return jnp.stack(came + goes + [lax.axis_index("y"), lax.axis_index("z")]).astype(jnp.int32)


def dot(a, b, dims=((1,), (0,))):
    return lax.dot_general(a, b, (dims, ((), ())), preferred_element_type=f32)


def load_weights(ids, weights, w, first, sem):
    copies = []
    for i, dy in enumerate(SHIFTS):
        copy = pltpu.make_async_copy(
            weights.at[:, i, :, pl.ds(first, w.shape[-1])], w.at[(ids[16] + 4 - dy) % 4], sem.at[i]
        )
        copy.start()
        copies.append(copy)
    return copies


def weights_by_layer(qkv_weight, out_t):
    first = jnp.concatenate([qkv_weight[0], out_t[0]], axis=1)
    first = jnp.concatenate([shifted(first, "y", s) for s in SHIFTS], axis=0)
    qkv_weight, out_t, first = lax.optimization_barrier((qkv_weight, out_t, first))
    shards = [jnp.concatenate([qkv_weight[l], out_t[l]], axis=1) for l in range(qkv_weight.shape[0])]
    held = jnp.concatenate(shards[1:], axis=0)
    later = [shifted(held, "y", s) for s in SHIFTS]
    columns = [first]
    for l in range(len(shards) - 1):
        columns.append(jnp.concatenate([p[64 * l : 64 * (l + 1)] for p in later], axis=0))
    return [lax.all_gather(c, "z", axis=0, tiled=True).reshape(8, 4, 64, 1024) for c in columns]


def project_kernel(layer, ids, *refs):
    parts, weights, refs = refs[:8], refs[8], refs[9:]
    gain, proj, qf_ref, kf_ref, v_ref, state_ref, w, scaled, squares, state, pair, low, sem = refs
    copies = load_weights(ids, weights, w, 0, sem)
    for n in range(2):
        part = proj[layer, n] * 128 ** (-0.25)
        high = part.astype(bf16)
        rest = part - high.astype(f32)
        mid = rest.astype(bf16)
        pair[n, :, :128] = high
        pair[n, :, 128:] = mid
        low[n] = (rest - mid.astype(f32)).astype(bf16)
    tokens = parts[0].shape[0]
    gains = [gain[pl.ds(layer * 8 + ids[k], 1), :] for k in range(8)]
    state[...] = jnp.zeros_like(state)

    @pl.loop(0, tokens // 64)
    def _(i):
        rows = pl.ds(pl.multiple_of(i * 64, 64), 64)
        total = jnp.zeros((64, 256), f32)
        for k in range(8):
            wide = parts[k][rows, :].astype(f32)
            total += wide * wide
            scaled[rows, pl.ds(pl.multiple_of(ids[k] * 256, 256), 256)] = (wide * gains[k]).astype(bf16)
        squares[rows, :] = total[:, :128] + total[:, 128:]

    for copy in copies:
        copy.wait()
    ones = jnp.ones((TILE, 128), bf16)

    @pl.loop(0, tokens // TILE)
    def _(i):
        rows = pl.ds(pl.multiple_of(i * TILE, TILE), TILE)
        inverse_rms = lax.rsqrt(jnp.sum(squares[rows, :], axis=-1, keepdims=True) * (1.0 / 2048) + 1e-05)
        qkv = (dot(scaled[rows, :], w[...].reshape(2048, 768)) * inverse_rms).astype(bf16)
        for n in range(2):
            feats = []
            for j in range(2):
                u = qkv[:, n * 384 + j * 128 : n * 384 + (j + 1) * 128]
                both = dot(u, pair[n])
                mixed = both[:, :128] + (both[:, 128:] + dot(u, low[n]))
                uw = u.astype(f32)
                energy = jnp.sum(uw * uw, axis=-1, keepdims=True) * (0.5 * 128 ** (-0.5))
                feats.append((jnp.exp(mixed - energy - STABILIZER) * 128 ** (-0.5)).astype(bf16))
            value = qkv[:, n * 384 + 256 : n * 384 + 384]
            cols = pl.ds(n * 128, 128)
            qf_ref[rows, cols] = feats[0]
            kf_ref[rows, cols] = feats[1]
            v_ref[rows, cols] = value
            state[cols, :] += dot(feats[1], jnp.concatenate([value, ones], axis=1), ((0,), (0,)))

    state_ref[...] = state[...].astype(bf16)


def project(layer, ids, parts, gain, w, proj):
    tokens = parts[0].shape[0]
    half = jax.ShapeDtypeStruct((tokens, 256), bf16)
    return pl.pallas_call(
        lambda *refs: project_kernel(layer, *refs),
        name="project",
        out_shape=(half, half, half, jax.ShapeDtypeStruct((256, 256), bf16)),
        in_specs=[SMEM] + [VMEM] * 8 + [HBM] + [VMEM] * 2,
        out_specs=(VMEM,) * 4,
        scratch_shapes=[
            pltpu.VMEM((4, 8, 64, 768), bf16),
            pltpu.VMEM((tokens, 2048), bf16),
            pltpu.VMEM((tokens, 128), f32),
            pltpu.VMEM((256, 256), f32),
            pltpu.VMEM((2, 128, 256), bf16),
            pltpu.VMEM((2, 128, 128), bf16),
            pltpu.SemaphoreType.DMA((4,)),
        ],
        cost_estimate=pl.CostEstimate(flops=2 * 512 * 2048 * 768, bytes_accessed=6 * 2**20, transcendentals=0),
        compiler_params=pltpu.CompilerParams(vmem_limit_bytes=LIMIT),
    )(ids, *parts, w, gain, proj)


def local_kernel(qf, kf, v, num_ref, den_ref):
    tile = 256
    keep = lax.broadcasted_iota(jnp.int32, (tile, tile), 0) >= lax.broadcasted_iota(jnp.int32, (tile, tile), 1)
    for n in range(2):
        cols = pl.ds(n * 128, 128)
        for i in range(qf.shape[0] // tile):
            rows = pl.ds(i * tile, tile)
            num = jnp.zeros((tile, 128), f32)
            den = jnp.zeros((tile, 1), f32)
            for j in range(i + 1):
                keys = pl.ds(j * tile, tile)
                scores = dot(qf[rows, cols], kf[keys, cols], ((1,), (1,)))
                if j == i:
                    scores = jnp.where(keep, scores, 0.0)
                den += jnp.sum(scores, axis=-1, keepdims=True)
                num += dot(scores.astype(bf16), v[keys, cols])
            num_ref[rows, cols] = num
            den_ref[rows, cols] = jnp.broadcast_to(den, (tile, 128))


def local_attention(qf, kf, v):
    whole = jax.ShapeDtypeStruct(qf.shape, f32)
    return pl.pallas_call(
        local_kernel,
        name="local_attention",
        out_shape=(whole, whole),
        in_specs=[VMEM] * 3,
        out_specs=(VMEM,) * 2,
        cost_estimate=pl.CostEstimate(flops=2 * 4 * 512 * 512 * 128, bytes_accessed=2 * 2**20, transcendentals=0),
        compiler_params=pltpu.CompilerParams(vmem_limit_bytes=LIMIT),
    )(qf, kf, v)


def prefix_kernel(peers, in_ref, out_ref):
    n = in_ref.shape[0]
    width = n // peers
    row = lax.broadcasted_iota(jnp.int32, (n, n), 0)
    col = lax.broadcasted_iota(jnp.int32, (n, n), 1)
    earlier = (col < (row & -width)) & (((row ^ col) & (width - 1)) == 0)
    out_ref[...] = dot(earlier.astype(f32).astype(bf16), in_ref[...]).astype(bf16)


def prefix(slices, peers):
    return pl.pallas_call(
        lambda *refs: prefix_kernel(peers, *refs),
        name="prefix",
        out_shape=jax.ShapeDtypeStruct(slices.shape, bf16),
        in_specs=[VMEM],
        out_specs=VMEM,
        compiler_params=pltpu.CompilerParams(vmem_limit_bytes=LIMIT),
    )(slices)


def finish_kernel(layer, ids, qf, num, den, before, gain, *refs):
    weights, outs = refs[0], refs[1:9]
    w, attended, sem = refs[-3:]
    copies = load_weights(ids, weights, w, 768, sem)

    for n in range(2):
        cols = pl.ds(n * 128, 128)
        both = dot(qf[:, cols], before[cols, :])
        attention = (num[:, cols] + both[:, :128]) / (den[:, cols] + both[:, 128:])
        inverse = lax.rsqrt(jnp.sum(attention * attention, axis=-1, keepdims=True) * (1.0 / 128) + 1e-06)
        attended[:, cols] = (attention * inverse * gain[pl.ds(layer, 1), cols]).astype(bf16)
    for copy in copies:
        copy.wait()
    for k in range(8):
        group = ids[8 + k]
        part = w[group // 2, pl.ds(group % 2 * 4, 4)].reshape(256, 256)
        outs[k][...] = dot(attended[...], part, ((1,), (1,))).astype(bf16)


def finish(layer, ids, qf, num, den, before, gain, w):
    part = jax.ShapeDtypeStruct(qf.shape, bf16)
    return pl.pallas_call(
        lambda *refs: finish_kernel(layer, *refs),
        name="finish",
        out_shape=(part,) * 8,
        in_specs=[SMEM] + [VMEM] * 5 + [HBM],
        out_specs=(VMEM,) * 8,
        scratch_shapes=[pltpu.VMEM((4, 8, 64, 256), bf16), pltpu.VMEM(qf.shape, bf16), pltpu.SemaphoreType.DMA((4,))],
        cost_estimate=pl.CostEstimate(flops=2 * 512 * 256 * 2304, bytes_accessed=5 * 2**20, transcendentals=0),
        compiler_params=pltpu.CompilerParams(vmem_limit_bytes=LIMIT),
    )(ids, qf, num, den, before, gain, w)


def gathered(own):
    mine = [shifted(own, "x", s) for s in SHIFTS]
    return mine + [swap(p) for p in mine]


def scattered(outs):
    sums = [m.astype(f32) + swap(o).astype(f32) for m, o in zip(outs[:4], outs[4:])]
    return sums[0] + sum(shifted(a.astype(bf16), "x", s).astype(f32) for a, s in zip(sums[1:], SHIFTS[1:]))


def local(hidden, qkv_weight, out_weight, projection, norm_gain, out_gain):
    layers = qkv_weight.shape[0]
    out_t = jnp.swapaxes(out_weight, 1, 2)
    weights = weights_by_layer(qkv_weight, out_t)
    ids = group_ids()
    gain = norm_gain.reshape(layers * 8, 256)
    peers = lax.axis_size(SEQ)
    stream = hidden
    for l in range(layers):
        qf, kf, v, state = project(l, ids, gathered(stream), gain, weights[l], projection)
        slices = lax.all_to_all(state.reshape(peers, 256 // peers, 256), SEQ, 0, 0, tiled=True).reshape(256, 256)
        num, den = local_attention(qf, kf, v)
        sums = prefix(slices, peers).reshape(peers, 256 // peers, 256)
        before = lax.all_to_all(sums, SEQ, 0, 0, tiled=True).reshape(256, 256)
        outs = finish(l, ids, qf, num, den, before, out_gain, weights[l])
        stream = (stream.astype(f32) + scattered(outs)).astype(bf16)
    return stream


def solution(mesh):
    finer = Mesh(mesh.devices.reshape(4, 8, X, 2), ("y", "z", "x", "c"))
    in_specs = (
        P(SEQ, GRP),
        P(None, SEQ, GRP),
        P(None, GRP, SEQ),
        P(None, GRP, None, None),
        P(),
        P(None, GRP),
    )
    return jax.shard_map(local, mesh=finer, in_specs=in_specs, out_specs=P(SEQ, GRP), check_vma=False)
```
